128 devices in a mesh: rows: 32 (over z, y, core), hosts: 4 (over x).
Axes of the slice: x: 4, y: 4, z: 4, core: 2. Of those that a mesh axis runs over, the one named last changes fastest.
Arguments:
- embeddings: float32 [131072, 768], P(('rows', 'hosts')), may hold values from -6 to 6
- root_centroids: float32 [512, 768], replicated, may hold values from -6 to 6
- member_ids: int32 [3, 131072], P(None, ('rows', 'hosts')), may hold values from 0 to 511
- split_order: int32 [3, 512], replicated, may hold values from 0 to 511, each once within a row
- seed_rows: int32 [3, 256, 2], replicated, may hold values from 0 to 131071
Outputs:
- centroids: float32 [512, 768], replicated
- spread: float32 [3, 512], replicated
- child_weight: float32 [3, 131072], P(None, ('rows', 'hosts'))
The draws below stay inside these ranges and needn't reach their ends.
Inputs may be any that keep to these rules, and one draw needn't show every extreme that they name: Each row of split_order names every cluster number once; its first 256 entries are the clusters split at that level.
All inputs are finite; a program needn't handle non-finite values.
Results may differ from the reference program's by a relative error of at most 0.0003.
Values sent between devices are 32-bit elements; how exact they have to be, the bound alone decides.
A program may use at most 64 MiB of HBM per device.

```python
import jax
import jax.numpy as jnp
from jax import lax

E = 768
SPLITS = 256
LEVELS = 3
CLUSTERS = 512
TOTAL_ROWS = 131072


def place_ends(entries, stream_key, least, top_value):
    extent = entries.shape
    place = [jax.random.randint(jax.random.fold_in(stream_key, axis), (), 0, extent[axis]) for axis in range(len(extent))]
    entries = entries.at[tuple(place)].set(least)
    longest = extent.index(max(extent))
    place[longest] = (place[longest] + 1) % extent[longest]
    return entries.at[tuple(place)].set(top_value)


def levels(key, shape, split, least, high):
    def one(dim, blocks):
        steps = jax.random.uniform(jax.random.fold_in(jax.random.fold_in(key, 6), dim), (blocks,), jnp.float32, least / len(split), high / len(split))
        return jnp.repeat(jnp.exp(steps), shape[dim] // blocks).reshape((-1,) + (1,) * (len(shape) - dim - 1))

    gain = one(*split[0])
    for cut in split[1:]:
        gain = gain * one(*cut)
    return gain


def noise(stream_key, dims, scale, bound, cuts=(), dtype=jnp.bfloat16):
    loudness = levels(stream_key, dims, cuts, -0.22, 0.18) if cuts else 1.0
    result = jax.random.normal(stream_key, dims, jnp.float32) * scale * loudness
    return jnp.minimum(jnp.maximum(result, -bound), bound).astype(dtype)


def setup_inputs(seed: int = 0) -> dict:
    key_of = jax.random.split(jax.random.key(seed), 6)
    embeddings = noise(key_of[0], (TOTAL_ROWS, E), 1.0, 6.0, ((0, 128),), jnp.float32)
    root_centroids = noise(key_of[1], (CLUSTERS, E), 1.0, 6.0, (), jnp.float32)
    member_ids = place_ends(jax.random.randint(key_of[2], (LEVELS, TOTAL_ROWS), 0, CLUSTERS), jax.random.fold_in(key_of[2], 1), 0, CLUSTERS - 1).astype(jnp.int32)
    split_order = jax.vmap(lambda own: jax.random.permutation(own, CLUSTERS))(jax.random.split(key_of[3], LEVELS)).reshape((LEVELS, CLUSTERS)).astype(jnp.int32)
    seed_rows = place_ends(jax.random.randint(key_of[4], (LEVELS, SPLITS, 2), 0, TOTAL_ROWS), jax.random.fold_in(key_of[4], 1), 0, TOTAL_ROWS - 1).astype(jnp.int32)
    return dict(embeddings=embeddings, root_centroids=root_centroids, member_ids=member_ids, split_order=split_order, seed_rows=seed_rows)


def reference(embeddings, root_centroids, member_ids, split_order, seed_rows):
    high = lax.Precision.HIGHEST
    width = embeddings.shape[1]
    scale = 0.5 / jnp.sqrt(jnp.float32(width))
    squares = lax.optimization_barrier(jnp.sum(embeddings * embeddings, axis=1))
    current = root_centroids
    spreads = []
    weights_out = []
    for level in range(LEVELS):
        splits = split_order[level, :SPLITS]
        parent = jnp.take(current, splits, axis=0)
        picked = jnp.take(embeddings, seed_rows[level], axis=0)
        seeds = 0.5 * (parent[:, None, :] + picked)
        delta = seeds[:, 0, :] - seeds[:, 1, :]
        offset = lax.optimization_barrier(jnp.sum(seeds[:, 1, :] ** 2, axis=1)) - lax.optimization_barrier(jnp.sum(seeds[:, 0, :] ** 2, axis=1))
        chosen = (member_ids[level][:, None] == splits[None, :]).astype(jnp.float32)
        projected = jnp.dot(embeddings, delta.T, precision=high)
        gap = lax.optimization_barrier(jnp.sum(chosen * (2.0 * projected + offset[None, :]), axis=1))
        first = jax.nn.sigmoid(gap * scale)
        inside = lax.optimization_barrier(jnp.sum(chosen, axis=1))
        weights_out.append(first * inside)
        weights = jnp.stack([chosen * first[:, None], chosen * (1.0 - first)[:, None]], axis=2)
        weights = weights.reshape(weights.shape[0], 2 * SPLITS)
        sums = lax.dot_general(weights, embeddings, (((0,), (0,)), ((), ())), precision=high)
        counts = lax.optimization_barrier(jnp.sum(weights, axis=0))
        energy = jnp.dot(squares, weights, precision=high)
        seeds_flat = seeds.reshape(2 * SPLITS, width)
        current = (sums + seeds_flat) / (counts + 1.0)[:, None]
        error = energy - 2.0 * lax.optimization_barrier(jnp.sum(current * sums, axis=1)) + counts * lax.optimization_barrier(jnp.sum(current * current, axis=1))
        spreads.append(error / ((counts + 1.0) * width))
    return (current, jnp.stack(spreads), jnp.stack(weights_out))
```

```python
import jax
import jax.numpy as jnp
from jax import lax
from jax.experimental import pallas as pl
from jax.experimental.pallas import tpu as pltpu
from jax.sharding import Mesh
from jax.sharding import PartitionSpec as P

F32 = jnp.float32
BF = jnp.bfloat16
I32 = jnp.int32
MESH = pl.DeviceIdType.MESH
HIGH = lax.Precision.HIGHEST

AXES = ("z", "y", "c", "x")
SIZE = {"z": 4, "y": 4, "c": 2, "x": 4}
ORDERS = (("x", "y", "z"), ("y", "z", "x"), ("z", "x", "y"))
PARTS = 3
ROWS = 1024
WIDTH = 768
SPLITS = 256
LEVELS = 3
KIDS = 512
TILE = 128


def two(value):
    high = value.astype(BF)
    return high, (value - high.astype(F32)).astype(BF)


def dot(a, b):
    return jnp.dot(a, b, preferred_element_type=F32)


def aligned(value, step):
    return pl.multiple_of(value, step)


class Links:
    def __init__(self):
        self.me = {a: lax.axis_index(a) for a in AXES}
        self.started = []

    def at(self, axis, step):
        return lax.rem(self.me[axis] + step, SIZE[axis])

    def send(self, src, dst, send_sem, recv_sem, device):
        copy = pltpu.make_async_remote_copy(
            src_ref=src, dst_ref=dst, send_sem=send_sem, recv_sem=recv_sem, device_id=device, device_id_type=MESH
        )
        copy.start()
        self.started.append(copy)
        return copy

    def drain(self):
        for copy in self.started:
            copy.wait_send()
        self.started = []


def near_group(links):
    return [{"x": links.at("x", i), "c": links.at("c", j)} for i in range(4) for j in range(2) if i or j]


def far_group(links):
    return [{"z": links.at("z", i), "y": links.at("y", j)} for i in range(4) for j in range(4) if i or j]


class AllSum:
    def __init__(self, links, near, far, sems):
        self.links, self.near, self.far, self.sems = links, near, far, sems

    def start(self, rows):
        links = self.links
        slot = links.me["x"] * 2 + links.me["c"]
        for i, row in enumerate(rows):
            self.near[slot, i : i + 1, :] = row
        if len(rows) < 8:
            self.near[slot, len(rows) :, :] = jnp.zeros((8 - len(rows), SPLITS), F32)
        mine = self.near.at[slot]
        self.waits = [
            links.send(mine, mine, self.sems.at[0, k], self.sems.at[1, k], device)
            for k, device in enumerate(near_group(links))
        ]

    def middle(self):
        links = self.links
        for copy in self.waits:
            copy.wait_recv()
        total = self.near[0]
        for k in range(1, 8):
            total = total + self.near[k]
        slot = links.me["z"] * 4 + links.me["y"]
        self.far[slot] = total
        mine = self.far.at[slot]
        self.waits = [
            links.send(mine, mine, self.sems.at[0, 7 + k], self.sems.at[1, 7 + k], device)
            for k, device in enumerate(far_group(links))
        ]

    def finish(self):
        for copy in self.waits:
            copy.wait_recv()
        total = self.far[0]
        for k in range(1, 16):
            total = total + self.far[k]
        return total


def add_into(dst, first, rows, sources, step):
    @pl.loop(0, rows // step)
    def _(i):
        at = pl.ds(aligned(first + i * step, step), step)
        total = dst[at, :]
        for source in sources:
            total = total + source[pl.ds(aligned(i * step, step), step), :]
        dst[at, :] = total


class Scatter:
    def __init__(self, links, data, core, one, two_, three, sems):
        self.links, self.data, self.sems = links, data, sems
        self.core, self.one, self.two, self.three = core, one, two_, three
        self.waits = None

    def send(self, q, k, src, dst, device):
        return self.links.send(src, dst, self.sems.at[0, q, k], self.sems.at[1, q, k], device)

    def wait(self):
        for copy in self.waits:
            copy.wait_recv()
        self.waits = []

    def start_core(self):
        links = self.links
        c = links.me["c"]
        self.waits = []
        for q in range(PARTS):
            src = self.data.at[pl.ds(aligned(256 * q + 128 * (1 - c), 128), 128), :]
            self.waits.append(self.send(q, 0, src, self.core.at[q], {"c": 1 - c}))

    def start_one(self):
        links = self.links
        self.wait()
        for q in range(PARTS):
            base = 256 * q + 128 * links.me["c"]
            add_into(self.data, base, 128, [self.core.at[q]], 16)
            axis = ORDERS[q][0]
            for k in range(1, 4):
                other = links.at(axis, k)
                src = self.data.at[pl.ds(aligned(base + 32 * other, 32), 32), :]
                self.waits.append(self.send(q, k, src, self.one.at[q, k - 1], {axis: other}))

    def start_two(self):
        links = self.links
        self.wait()
        for q in range(PARTS):
            base = 256 * q + 128 * links.me["c"] + 32 * links.me[ORDERS[q][0]]
            add_into(self.data, base, 32, [self.one.at[q, k] for k in range(3)], 8)
            axis = ORDERS[q][1]
            for k in range(1, 4):
                other = links.at(axis, k)
                src = self.data.at[pl.ds(aligned(base + 8 * other, 8), 8), :]
                self.waits.append(self.send(q, 3 + k, src, self.two.at[q, k - 1], {axis: other}))

    def start_three(self):
        links = self.links
        self.wait()
        for q in range(PARTS):
            base = own_row(links, q)
            axis = ORDERS[q][2]
            slot = links.me[axis]
            total = self.data[pl.ds(aligned(base, 8), 8), :]
            for k in range(3):
                total = total + self.two[q, k]
            self.three[q, slot] = total
            mine = self.three.at[q, slot]
            for k in range(1, 4):
                self.waits.append(self.send(q, 6 + k, mine, mine, {axis: links.at(axis, k)}))

    def finish(self):
        self.wait()
        return [
            ((self.three[q, 0] + self.three[q, 1]) + self.three[q, 2]) + self.three[q, 3] for q in range(PARTS)
        ]


def own_row(links, q):
    first, second, _ = ORDERS[q]
    return 256 * q + 128 * links.me["c"] + 32 * links.me[first] + 8 * links.me[second]


class Gather:
    def __init__(self, links, data, sems):
        self.links, self.data, self.sems = links, data, sems

    def push(self, q, k, base, rows, device):
        block = self.data.at[pl.ds(aligned(base, rows), rows), :]
        return self.links.send(block, block, self.sems.at[0, q, k], self.sems.at[1, q, k], device)

    def wait(self):
        for copy in self.waits:
            copy.wait_recv()
        self.waits = []

    def start_two(self, own):
        links = self.links
        self.waits = []
        for q in range(PARTS):
            base = own_row(links, q)
            self.data[pl.ds(aligned(base, 8), 8), :] = own[q]
            axis = ORDERS[q][1]
            for k in range(1, 4):
                self.waits.append(self.push(q, k, base, 8, {axis: links.at(axis, k)}))

    def start_one(self):
        links = self.links
        self.wait()
        for q in range(PARTS):
            base = 256 * q + 128 * links.me["c"] + 32 * links.me[ORDERS[q][0]]
            axis = ORDERS[q][0]
            for k in range(1, 4):
                self.waits.append(self.push(q, 3 + k, base, 32, {axis: links.at(axis, k)}))

    def start_core(self):
        links = self.links
        self.wait()
        c = links.me["c"]
        for q in range(PARTS):
            self.waits.append(self.push(q, 0, 256 * q + 128 * c, 128, {"c": 1 - c}))

    def finish(self):
        self.wait()


def pick(index, columns):
    hit = lax.broadcasted_iota(I32, (SPLITS, SPLITS), 0) == index
    return [jnp.sum(jnp.where(hit, column, 0), axis=0, keepdims=True) for column in columns]


def kernel(e_ref, root_ref, mem_ref, tabr_ref, tabc_ref, cent_ref, spread_ref, cw_ref, *scratch):
    (
        eh, el, eth, etl, rh, rl, roott, oh, w_lo, dh, dl, proj, sq, cwbuf,
        xd, x0, x1, x2, df, cf,
        core_d, core_0, core_1, core_2,
        one_d, one_0, one_1, one_2,
        two_d, two_0, two_1, two_2,
        three_d, three_0, three_1, three_2,
        near, far, woven, sem_rs, sem_ag, sem_ar,
    ) = scratch
    w_hi = oh
    links = Links()
    me = links.me
    barrier = pltpu.get_barrier_semaphore()
    peers = near_group(links) + far_group(links)
    for device in peers:
        pl.semaphore_signal(barrier, inc=1, device_id=device, device_id_type=MESH)

    rs_d = Scatter(links, xd, core_d, one_d, two_d, three_d, sem_rs.at[0])
    rs_0 = Scatter(links, x0, core_0, one_0, two_0, three_0, sem_rs.at[1])
    rs_1 = Scatter(links, x1, core_1, one_1, two_1, three_1, sem_rs.at[2])
    rs_2 = Scatter(links, x2, core_2, one_2, two_2, three_2, sem_rs.at[3])
    ag_d = Gather(links, df, sem_ag.at[0])
    ag_c = Gather(links, cf, sem_ag.at[1])
    sums = [AllSum(links, near.at[i], far.at[i], sem_ar.at[i]) for i in range(5)]

    first_row = (me["z"] * 32 + me["y"] * 8 + me["c"] * 4 + me["x"]) * ROWS

    @pl.loop(0, ROWS // TILE)
    def _(i):
        at = pl.ds(aligned(i * TILE, TILE), TILE)
        rows = e_ref[at, :]
        high, low = two(rows)
        eh[at, :] = high
        el[at, :] = low
        sq[at, :] = jnp.sum(rows * rows, axis=1, keepdims=True)
        turned = jnp.transpose(rows)
        high, low = two(turned)
        eth[:, at] = high
        etl[:, at] = low

    splits = [tabr_ref[l : l + 1, :] for l in range(LEVELS)]
    seed = [[tabr_ref[3 + 3 * j + l : 4 + 3 * j + l, :] - first_row for j in range(2)] for l in range(LEVELS)]

    def place(sign, with_norm):
        zero = jnp.zeros((1, SPLITS), F32)

        def body(i, carry):
            at = pl.ds(aligned(i * TILE, TILE), TILE)
            row = lax.broadcasted_iota(I32, (TILE, SPLITS), 0) + i * TILE
            out = []
            for l in range(LEVELS):
                value = jnp.where(row == seed[l][0], 1.0, 0.0) + jnp.where(row == seed[l][1], sign, 0.0)
                oh[at, l * SPLITS : (l + 1) * SPLITS] = value.astype(BF)
                if with_norm:
                    out.append(carry[l] + jnp.sum(value * sq[at, :], axis=0, keepdims=True))
            return tuple(out) if with_norm else carry

        return lax.fori_loop(0, ROWS // TILE, body, (zero,) * LEVELS)

    def select_rows(dst, first_col):
        @pl.loop(0, WIDTH // 256)
        def _(i):
            at = pl.ds(aligned(i * 256, 256), 256)
            dst[at, first_col : first_col + WIDTH] = dot(eth[at, :], oh[...]) + dot(etl[at, :], oh[...])

    norms = place(-1.0, True)
    select_rows(xd, 0)

    pl.semaphore_wait(barrier, len(peers))
    rs_d.start_core()
    sums[0].start(list(norms))

    col = [tabc_ref[:, k : k + 1] for k in range(6)]
    kid1 = splits[1]
    a1, s10, s11 = pick(kid1 >> 1, [col[0], col[2], col[3]])
    odd1 = (kid1 & 1) == 1
    seed1 = jnp.where(odd1, s11, s10) - first_row
    kid2 = splits[2]
    mid2, s20, s21 = pick(kid2 >> 1, [col[1], col[4], col[5]])
    odd2 = (kid2 & 1) == 1
    seed2 = jnp.where(odd2, s21, s20) - first_row
    a2, t20, t21 = pick(mid2 >> 1, [col[0], col[2], col[3]])
    odd20 = (mid2 & 1) == 1
    seed20 = jnp.where(odd20, t21, t20) - first_row

    @pl.loop(0, KIDS // TILE)
    def _(i):
        at = pl.ds(aligned(i * TILE, TILE), TILE)
        rows = root_ref[at, :]
        high, low = two(rows)
        rh[at, :] = high
        rl[at, :] = low
        roott[:, at] = jnp.transpose(rows)

    rs_d.start_one()
    place(1.0, False)
    sums[0].middle()
    rs_d.start_two()
    rs_d.start_three()
    own_d = jnp.concatenate(rs_d.finish(), axis=0)
    ag_d.start_two([own_d[8 * q : 8 * q + 8] for q in range(PARTS)])
    ag_d.start_one()
    ag_d.start_core()
    select_rows(x0, KIDS)
    norm = sums[0].finish()
    ag_d.finish()

    @pl.loop(0, WIDTH // TILE)
    def _(i):
        at = pl.ds(aligned(i * TILE, TILE), TILE)
        high, low = two(df[at, :])
        dh[at, :] = high
        dl[at, :] = low

    @pl.loop(0, ROWS // 256)
    def _(i):
        at = pl.ds(aligned(i * 256, 256), 256)
        proj[at, :] = dot(eh[at, :], dh[...]) + dot(eh[at, :], dl[...]) + dot(el[at, :], dh[...])

    def root_body(i, carry):
        at = pl.ds(aligned(i * TILE, TILE), TILE)
        value = dot(rh[at, :], dh[...]) + dot(rh[at, :], dl[...]) + dot(rl[at, :], dh[...])
        row = lax.broadcasted_iota(I32, (TILE, SPLITS), 0) + i * TILE
        return tuple(
            carry[l] + jnp.sum(jnp.where(row == index, value[:, l * SPLITS : (l + 1) * SPLITS], 0.0), axis=0, keepdims=True)
            for l, index in enumerate((splits[0], a1, a2))
        )

    along = lax.fori_loop(0, KIDS // TILE, root_body, (jnp.zeros((1, SPLITS), F32),) * LEVELS)

    scale = 0.5 / float(WIDTH) ** 0.5

    def level(l, offset, chains):
        zero = jnp.zeros((1, SPLITS), F32)

        def body(i, carry):
            at = pl.ds(aligned(i * TILE, TILE), TILE)
            member = mem_ref[at, l : l + 1]
            squares = sq[at, :]
            hit = member == splits[l]
            value = proj[at, l * SPLITS : (l + 1) * SPLITS] + offset
            gap = jnp.sum(jnp.where(hit, value, 0.0), axis=1, keepdims=True)
            inside = jnp.sum(jnp.where(hit, 1.0, 0.0), axis=1, keepdims=True)
            first = lax.logistic(gap * scale)
            second = 1.0 - first
            cwbuf[at, l : l + 1] = first * inside
            out = []
            for j, part in enumerate((first, second)):
                weight = jnp.where(hit, part, 0.0)
                high, low = two(weight)
                w_hi[at, j * SPLITS : (j + 1) * SPLITS] = high
                w_lo[at, j * SPLITS : (j + 1) * SPLITS] = low
                out.append(jnp.sum(weight, axis=0, keepdims=True))
                out.append(jnp.sum(weight * squares, axis=0, keepdims=True))
            row = lax.broadcasted_iota(I32, (TILE, SPLITS), 0) + i * TILE
            for cluster, odd, seed_row, ahead in chains:
                weight = jnp.where(member == cluster, jnp.where(odd, second, first), 0.0)
                both = weight + jnp.where(row == seed_row, 0.5, 0.0)
                out.append(jnp.sum(both * proj[at, ahead * SPLITS : (ahead + 1) * SPLITS], axis=0, keepdims=True))
                out.append(jnp.sum(weight, axis=0, keepdims=True))
            return tuple(a + b for a, b in zip(carry, out))

        return list(lax.fori_loop(0, ROWS // TILE, body, (zero,) * (4 + 2 * len(chains))))

    def add_up(dst):
        @pl.loop(0, WIDTH // 256)
        def _(i):
            at = pl.ds(aligned(i * 256, 256), 256)
            wide = w_hi[:, :KIDS]
            dst[at, :KIDS] = dot(eth[at, :], wide) + dot(etl[at, :], wide) + dot(eth[at, :], w_lo[...])

    offset = -0.5 * along[0] - 0.25 * norm[0:1, :]
    sums[1].start(level(0, offset, [(a1, odd1, seed1, 1), (a2, odd20, seed20, 2)]))
    add_up(x0)
    rs_0.start_core()
    sums[1].middle()
    rs_0.start_one()
    got0 = sums[1].finish()

    parent = (got0[4:5, :] + 0.5 * along[1]) / (got0[5:6, :] + 1.0)
    offset = -0.5 * parent - 0.25 * norm[1:2, :]
    sums[2].start(level(1, offset, [(mid2, odd2, seed2, 2)]))
    add_up(x1)
    rs_1.start_core()
    sums[2].middle()
    rs_0.start_two()
    rs_1.start_one()
    got1 = sums[2].finish()

    older = (got0[6:7, :] + 0.5 * along[2]) / (got0[7:8, :] + 1.0)
    parent = (got1[4:5, :] + 0.5 * older) / (got1[5:6, :] + 1.0)
    offset = -0.5 * parent - 0.25 * norm[2:3, :]
    sums[3].start(level(2, offset, []))
    add_up(x2)
    rs_2.start_core()
    sums[3].middle()
    rs_0.start_three()
    rs_1.start_two()
    rs_2.start_one()
    got2 = sums[3].finish()
    own_0 = jnp.concatenate(rs_0.finish(), axis=0)
    rs_1.start_three()
    rs_2.start_two()

    def rows_of_root():
        return jnp.concatenate([roott[pl.ds(aligned(own_row(links, q), 8), 8), :] for q in range(PARTS)], axis=0)

    def child(l, got, mine, from_, kid):
        line = lax.broadcasted_iota(I32, (KIDS, SPLITS), 0)
        parent = jnp.dot(
            from_, jnp.where(line == kid, 1.0, 0.0).astype(F32), precision=HIGH, preferred_element_type=F32
        )
        up = own_0[:, KIDS + l * SPLITS : KIDS + (l + 1) * SPLITS]
        diff = own_d[:, l * SPLITS : (l + 1) * SPLITS]
        seeds = 0.5 * jnp.concatenate([parent + 0.5 * (up + diff), parent + 0.5 * (up - diff)], axis=1)
        count = jnp.concatenate([got[0:1, :], got[2:3, :]], axis=1)
        centre = (mine + seeds) / (count + 1.0)
        error = jnp.sum(count * centre * centre - 2.0 * centre * mine, axis=0, keepdims=True)
        return centre, 0.25 * error, count

    def flat(kid):
        return (kid & 1) * SPLITS + (kid >> 1)

    c1, err0, n0 = child(0, got0, own_0[:, :KIDS], rows_of_root(), splits[0])
    own_1 = jnp.concatenate(rs_1.finish(), axis=0)
    rs_2.start_three()
    c2, err1, n1 = child(1, got1, own_1, c1, flat(kid1))
    own_2 = jnp.concatenate(rs_2.finish(), axis=0)
    c3, err2, n2 = child(2, got2, own_2, c2, flat(kid2))
    ag_c.start_two([c3[8 * q : 8 * q + 8] for q in range(PARTS)])
    sums[4].start([e[:, j * SPLITS : (j + 1) * SPLITS] for e in (err0, err1, err2) for j in range(2)])
    ag_c.start_one()
    sums[4].middle()
    ag_c.start_core()
    cw_ref[...] = jnp.transpose(cwbuf[...])[0:LEVELS]
    total = sums[4].finish()
    lines = []
    for l, (got, n) in enumerate(((got0, n0), (got1, n1), (got2, n2))):
        energy = jnp.concatenate([got[1:2, :], got[3:4, :]], axis=1)
        error = jnp.concatenate([total[2 * l : 2 * l + 1, :], total[2 * l + 1 : 2 * l + 2, :]], axis=1)
        lines.append((energy + error) / ((n + 1.0) * WIDTH))
    lines.append(jnp.zeros((8 - LEVELS, KIDS), F32))
    line = lax.broadcasted_iota(I32, (KIDS, KIDS), 0)
    kid = lax.broadcasted_iota(I32, (KIDS, KIDS), 1)
    order = jnp.where(line == flat(kid), 1.0, 0.0).astype(F32)
    spread_ref[...] = jnp.dot(
        jnp.concatenate(lines, axis=0), order, precision=HIGH, preferred_element_type=F32
    )[0:LEVELS]
    ag_c.finish()
    for w in range(WIDTH // TILE):
        for j in range(2):
            block = jnp.transpose(cf[w * TILE : (w + 1) * TILE, j * SPLITS : (j + 1) * SPLITS])
            woven[w, pl.ds(j, SPLITS, stride=2), :] = block
        cent_ref[:, w * TILE : (w + 1) * TILE] = woven[w]
    links.drain()


def scratch_shapes():
    vm = pltpu.VMEM
    widths = (WIDTH, KIDS + WIDTH, KIDS, KIDS)
    shapes = [
        vm((ROWS, WIDTH), BF), vm((ROWS, WIDTH), BF), vm((WIDTH, ROWS), BF), vm((WIDTH, ROWS), BF),
        vm((KIDS, WIDTH), BF), vm((KIDS, WIDTH), BF), vm((WIDTH, KIDS), F32),
        vm((ROWS, WIDTH), BF), vm((ROWS, KIDS), BF),
        vm((WIDTH, WIDTH), BF), vm((WIDTH, WIDTH), BF), vm((ROWS, WIDTH), F32),
        vm((ROWS, 1), F32), vm((ROWS, 128), F32),
    ]
    shapes += [vm((WIDTH, n), F32) for n in widths]
    shapes += [vm((WIDTH, WIDTH), F32), vm((WIDTH, KIDS), F32)]
    shapes += [vm((PARTS, 128, n), F32) for n in widths]
    shapes += [vm((PARTS, 3, 32, n), F32) for n in widths]
    shapes += [vm((PARTS, 3, 8, n), F32) for n in widths]
    shapes += [vm((PARTS, 4, 8, n), F32) for n in widths]
    dma = pltpu.SemaphoreType.DMA
    shapes += [vm((5, 8, 8, SPLITS), F32), vm((5, 16, 8, SPLITS), F32)]
    shapes += [vm((WIDTH // TILE, KIDS, TILE), F32)]
    shapes += [dma((4, 2, PARTS, 10)), dma((2, 2, PARTS, 7)), dma((5, 2, 22))]
    return shapes


def on_device(embeddings, root_centroids, member_ids, split_order, seed_rows):
    table = jnp.concatenate(
        [split_order[:, :SPLITS], seed_rows[:, :, 0], seed_rows[:, :, 1], jnp.zeros((7, SPLITS), I32)], axis=0
    )
    columns = jnp.stack(
        [
            split_order[0, :SPLITS], split_order[1, :SPLITS],
            seed_rows[0, :, 0], seed_rows[0, :, 1], seed_rows[1, :, 0], seed_rows[1, :, 1],
        ],
        axis=1,
    )
    member = member_ids.T
    vmem = pl.BlockSpec(memory_space=pltpu.VMEM)
    return pl.pallas_call(
        kernel,
        out_shape=(
            jax.ShapeDtypeStruct((KIDS, WIDTH), F32),
            jax.ShapeDtypeStruct((LEVELS, KIDS), F32),
            jax.ShapeDtypeStruct((LEVELS, ROWS), F32),
        ),
        in_specs=[vmem] * 5,
        out_specs=(vmem,) * 3,
        scratch_shapes=scratch_shapes(),
        compiler_params=pltpu.CompilerParams(
            collective_id=0, has_side_effects=True, vmem_limit_bytes=66_000_000
        ),
    )(embeddings, root_centroids, member, table, columns)


def solution(mesh):
    split = Mesh(mesh.devices.reshape(4, 4, 2, 4), AXES)
    everywhere = ("z", "y", "c", "x")
    in_specs = (P(everywhere, None), P(), P(None, everywhere), P(), P())
    out_specs = (P(), P(), P(None, everywhere))
    return jax.shard_map(on_device, mesh=split, in_specs=in_specs, out_specs=out_specs, check_vma=False)
```

```python
import jax
import jax.numpy as jnp
from jax import lax
from jax.experimental import pallas as pl
from jax.experimental.pallas import tpu as pltpu
from jax.sharding import Mesh
from jax.sharding import PartitionSpec as P

F32 = jnp.float32
BF = jnp.bfloat16
I32 = jnp.int32
MESH = pl.DeviceIdType.MESH
HIGH = lax.Precision.HIGHEST

AXES = ("z", "y", "c", "x")
SIZE = {"z": 4, "y": 4, "c": 2, "x": 4}
ORDERS = (("x", "y", "z"), ("y", "z", "x"), ("z", "x", "y"))
PARTS = 3
ROWS = 1024
WIDTH = 768
SPLITS = 256
LEVELS = 3
FAR_FIRST = (2, 1, 3)
KIDS = 512
TILE = 128


def two(value):
    high = value.astype(BF)
    return high, (value - high.astype(F32)).astype(BF)


def dot(a, b):
    return jnp.dot(a, b, preferred_element_type=F32)


def aligned(value, step):
    return pl.multiple_of(value, step)


class Links:
    def __init__(self):
        self.me = {a: lax.axis_index(a) for a in AXES}
        self.started = []

    def at(self, axis, step):
        return lax.rem(self.me[axis] + step, SIZE[axis])

    def send(self, src, dst, send_sem, recv_sem, device):
        copy = pltpu.make_async_remote_copy(
            src_ref=src, dst_ref=dst, send_sem=send_sem, recv_sem=recv_sem, device_id=device, device_id_type=MESH
        )
        copy.start()
        self.started.append(copy)
        return copy

    def drain(self):
        for copy in self.started:
            copy.wait_send()
        self.started = []


def near_group(links):
    return [{"x": links.at("x", i), "c": links.at("c", j)} for i in range(4) for j in range(2) if i or j]


def far_group(links):
    return [{"z": links.at("z", i), "y": links.at("y", j)} for i in range(4) for j in range(4) if i or j]


class AllSum:
    def __init__(self, links, near, far, sems):
        self.links, self.near, self.far, self.sems = links, near, far, sems

    def start(self, rows):
        links = self.links
        slot = links.me["x"] * 2 + links.me["c"]
        for i, row in enumerate(rows):
            self.near[slot, i : i + 1, :] = row
        if len(rows) < 8:
            self.near[slot, len(rows) :, :] = jnp.zeros((8 - len(rows), SPLITS), F32)
        mine = self.near.at[slot]
        self.waits = [
            links.send(mine, mine, self.sems.at[0, k], self.sems.at[1, k], device)
            for k, device in enumerate(near_group(links))
        ]

    def middle(self):
        links = self.links
        for copy in self.waits:
            copy.wait_recv()
        total = self.near[0]
        for k in range(1, 8):
            total = total + self.near[k]
        slot = links.me["z"] * 4 + links.me["y"]
        self.far[slot] = total
        mine = self.far.at[slot]
        self.waits = [
            links.send(mine, mine, self.sems.at[0, 7 + k], self.sems.at[1, 7 + k], device)
            for k, device in enumerate(far_group(links))
        ]

    def finish(self):
        for copy in self.waits:
            copy.wait_recv()
        total = self.far[0]
        for k in range(1, 16):
            total = total + self.far[k]
        return total


def add_into(dst, first, rows, sources, step):
    @pl.loop(0, rows // step)
    def _(i):
        at = pl.ds(aligned(first + i * step, step), step)
        total = dst[at, :]
        for source in sources:
            total = total + source[pl.ds(aligned(i * step, step), step), :]
        dst[at, :] = total


class Scatter:
    def __init__(self, links, data, core, one, two_, three, sems):
        self.links, self.data, self.sems = links, data, sems
        self.core, self.one, self.two, self.three = core, one, two_, three
        self.waits = [[] for _ in range(PARTS)]

    def send(self, q, k, src, dst, device):
        self.waits[q].append(self.links.send(src, dst, self.sems.at[0, q, k], self.sems.at[1, q, k], device))

    def wait(self, q):
        for copy in self.waits[q]:
            copy.wait_recv()
        self.waits[q] = []

    def start_core(self, q):
        other = 1 - self.links.me["c"]
        src = self.data.at[pl.ds(aligned(256 * q + 128 * other, 128), 128), :]
        self.send(q, 0, src, self.core.at[q], {"c": other})

    def start_one(self):
        links = self.links
        for q in range(PARTS):
            self.wait(q)
            base = 256 * q + 128 * links.me["c"]
            add_into(self.data, base, 128, [self.core.at[q]], 16)
            axis = ORDERS[q][0]
            for k in FAR_FIRST:
                other = links.at(axis, k)
                src = self.data.at[pl.ds(aligned(base + 32 * other, 32), 32), :]
                self.send(q, k, src, self.one.at[q, k - 1], {axis: other})

    def start_two(self):
        links = self.links
        for q in range(PARTS):
            self.wait(q)
            base = 256 * q + 128 * links.me["c"] + 32 * links.me[ORDERS[q][0]]
            add_into(self.data, base, 32, [self.one.at[q, k] for k in range(3)], 8)
            axis = ORDERS[q][1]
            for k in FAR_FIRST:
                other = links.at(axis, k)
                src = self.data.at[pl.ds(aligned(base + 8 * other, 8), 8), :]
                self.send(q, 3 + k, src, self.two.at[q, k - 1], {axis: other})

    def start_three(self):
        links = self.links
        for q in range(PARTS):
            self.wait(q)
            base = own_row(links, q)
            axis = ORDERS[q][2]
            slot = links.me[axis]
            total = self.data[pl.ds(aligned(base, 8), 8), :]
            for k in range(3):
                total = total + self.two[q, k]
            self.three[q, slot] = total
            mine = self.three.at[q, slot]
            for k in FAR_FIRST:
                self.send(q, 6 + k, mine, mine, {axis: links.at(axis, k)})

    def finish(self, q):
        self.wait(q)
        return ((self.three[q, 0] + self.three[q, 1]) + self.three[q, 2]) + self.three[q, 3]

    def finish_all(self):
        return jnp.concatenate([self.finish(q) for q in range(PARTS)], axis=0)


def own_row(links, q):
    first, second, _ = ORDERS[q]
    return 256 * q + 128 * links.me["c"] + 32 * links.me[first] + 8 * links.me[second]


class Gather:
    def __init__(self, links, data, sems):
        self.links, self.data, self.sems = links, data, sems
        self.waits = [[] for _ in range(PARTS)]

    def push(self, q, k, base, rows, device):
        block = self.data.at[pl.ds(aligned(base, rows), rows), :]
        self.waits[q].append(self.links.send(block, block, self.sems.at[0, q, k], self.sems.at[1, q, k], device))

    def wait(self, q):
        for copy in self.waits[q]:
            copy.wait_recv()
        self.waits[q] = []

    def start_two(self, q, own):
        links = self.links
        base = own_row(links, q)
        self.data[pl.ds(aligned(base, 8), 8), :] = own
        axis = ORDERS[q][1]
        for k in FAR_FIRST:
            self.push(q, k, base, 8, {axis: links.at(axis, k)})

    def start_one(self):
        links = self.links
        for q in range(PARTS):
            self.wait(q)
            base = 256 * q + 128 * links.me["c"] + 32 * links.me[ORDERS[q][0]]
            axis = ORDERS[q][0]
            for k in FAR_FIRST:
                self.push(q, 3 + k, base, 32, {axis: links.at(axis, k)})

    def start_core(self):
        c = self.links.me["c"]
        for q in range(PARTS):
            self.wait(q)
            self.push(q, 0, 256 * q + 128 * c, 128, {"c": 1 - c})


def pick(index, columns):
    hit = lax.broadcasted_iota(I32, (SPLITS, SPLITS), 0) == index
    return [jnp.sum(jnp.where(hit, column, 0.0), axis=0, keepdims=True).astype(I32) for column in columns]


def kernel(e_hbm, root_hbm, mem_ref, split_ref, seed_ref, cent_hbm, spread_ref, cw_ref, *scratch):
    (
        e_ref, root_ref,
        eh, el, eth, etl, rh, rl, roott, oh, w_lo, dh, dl, proj, sq, memc, colt, cwbuf,
        xd, xu, x0, x1, x2, df, cf,
        core_d, core_u, core_0, core_1, core_2,
        one_d, one_u, one_0, one_1, one_2,
        two_d, two_u, two_0, two_1, two_2,
        three_d, three_u, three_0, three_1, three_2,
        near, far, woven, sem_rs, sem_ag, sem_ar, sem_in, sem_out,
    ) = scratch
    w_hi = oh
    links = Links()
    me = links.me
    barrier = pltpu.get_barrier_semaphore()
    peers = near_group(links) + far_group(links)
    for device in peers:
        pl.semaphore_signal(barrier, inc=1, device_id=device, device_id_type=MESH)

    tiles = ROWS // TILE

    def fetch(i):
        at = pl.ds(aligned(i * TILE, TILE), TILE)
        return pltpu.make_async_copy(e_hbm.at[at, :], e_ref.at[at, :], sem_in.at[i])

    root_copy = pltpu.make_async_copy(root_hbm, root_ref, sem_in.at[tiles])
    for i in range(tiles):
        fetch(i).start()
    root_copy.start()

    rs_d = Scatter(links, xd, core_d, one_d, two_d, three_d, sem_rs.at[0])
    rs_u = Scatter(links, xu, core_u, one_u, two_u, three_u, sem_rs.at[1])
    rs_0 = Scatter(links, x0, core_0, one_0, two_0, three_0, sem_rs.at[2])
    rs_1 = Scatter(links, x1, core_1, one_1, two_1, three_1, sem_rs.at[3])
    rs_2 = Scatter(links, x2, core_2, one_2, two_2, three_2, sem_rs.at[4])
    ag_d = Gather(links, df, sem_ag.at[0])
    ag_c = Gather(links, cf, sem_ag.at[1])
    sums = [AllSum(links, near.at[i], far.at[i], sem_ar.at[i]) for i in range(5)]

    first_row = (me["z"] * 32 + me["y"] * 8 + me["c"] * 4 + me["x"]) * ROWS
    splits = [split_ref[l : l + 1, :SPLITS] for l in range(LEVELS)]
    seed = [[seed_ref[l, j : j + 1, :] - first_row for j in range(2)] for l in range(LEVELS)]

    @pl.loop(0, tiles)
    def _(i):
        fetch(i).wait()
        at = pl.ds(aligned(i * TILE, TILE), TILE)
        rows = e_ref[at, :]
        high, low = two(rows)
        eh[at, :] = high
        el[at, :] = low
        sq[at, :] = jnp.sum(rows * rows, axis=1, keepdims=True)
        turned = jnp.transpose(rows)
        high, low = two(turned)
        eth[:, at] = high
        etl[:, at] = low

    def place(sign, with_norm):
        zero = jnp.zeros((1, SPLITS), F32)

        def body(i, carry):
            at = pl.ds(aligned(i * TILE, TILE), TILE)
            row = lax.broadcasted_iota(I32, (TILE, SPLITS), 0) + i * TILE
            out = []
            for l in range(LEVELS):
                value = jnp.where(row == seed[l][0], 1.0, 0.0) + jnp.where(row == seed[l][1], sign, 0.0)
                oh[at, l * SPLITS : (l + 1) * SPLITS] = value.astype(BF)
                if with_norm:
                    out.append(carry[l] + jnp.sum(value * sq[at, :], axis=0, keepdims=True))
            return tuple(out) if with_norm else carry

        return lax.fori_loop(0, tiles, body, (zero,) * LEVELS)

    def select_rows(dst, q):
        at = slice(256 * q, 256 * q + 256)
        dst[at, :] = dot(eth[at, :], oh[...]) + dot(etl[at, :], oh[...])

    norms = place(-1.0, True)
    select_rows(xd, 0)
    pl.semaphore_wait(barrier, len(peers))
    rs_d.start_core(0)
    sums[0].start(list(norms))
    for q in (1, 2):
        select_rows(xd, q)
        rs_d.start_core(q)

    lines = [splits[0], splits[1], seed_ref[0, 0:1, :], seed_ref[0, 1:2, :], seed_ref[1, 0:1, :], seed_ref[1, 1:2, :]]
    lines = [line.astype(F32) for line in lines] + [jnp.zeros((TILE - 6, SPLITS), F32)]
    colt[...] = jnp.transpose(jnp.concatenate(lines, axis=0))
    memc[...] = jnp.transpose(
        jnp.concatenate([mem_ref[...].astype(F32), jnp.zeros((TILE - LEVELS, ROWS), F32)], axis=0)
    )
    col = [colt[:, k : k + 1] for k in range(6)]
    kid1 = splits[1]
    a1, s10, s11 = pick(kid1 >> 1, [col[0], col[2], col[3]])
    odd1 = (kid1 & 1) == 1
    seed1 = jnp.where(odd1, s11, s10) - first_row
    kid2 = splits[2]
    mid2, s20, s21 = pick(kid2 >> 1, [col[1], col[4], col[5]])
    odd2 = (kid2 & 1) == 1
    seed2 = jnp.where(odd2, s21, s20) - first_row
    a2, t20, t21 = pick(mid2 >> 1, [col[0], col[2], col[3]])
    odd20 = (mid2 & 1) == 1
    seed20 = jnp.where(odd20, t21, t20) - first_row
    rs_d.start_one()

    root_copy.wait()

    @pl.loop(0, KIDS // TILE)
    def _(i):
        at = pl.ds(aligned(i * TILE, TILE), TILE)
        rows = root_ref[at, :]
        high, low = two(rows)
        rh[at, :] = high
        rl[at, :] = low
        roott[:, at] = jnp.transpose(rows)

    place(1.0, False)
    sums[0].middle()
    rs_d.start_two()
    select_rows(xu, 0)
    rs_d.start_three()
    select_rows(xu, 1)
    own_d = []
    for q in range(PARTS):
        own_d.append(rs_d.finish(q))
        ag_d.start_two(q, own_d[q])
    own_d = jnp.concatenate(own_d, axis=0)
    select_rows(xu, 2)
    ag_d.start_one()
    norm = sums[0].finish()
    ag_d.start_core()
    for q in range(PARTS):
        rs_u.start_core(q)

    for q in range(PARTS):
        ag_d.wait(q)
        for i in range(2):
            at = slice(256 * q + 128 * i, 256 * q + 128 * (i + 1))
            high, low = two(df[at, :])
            dh[at, :] = high
            dl[at, :] = low

    @pl.loop(0, ROWS // 256)
    def _(i):
        at = pl.ds(aligned(i * 256, 256), 256)
        proj[at, :] = dot(eh[at, :], dh[...]) + dot(eh[at, :], dl[...]) + dot(el[at, :], dh[...])

    rs_u.start_one()

    def root_body(i, carry):
        at = pl.ds(aligned(i * TILE, TILE), TILE)
        value = dot(rh[at, :], dh[...]) + dot(rh[at, :], dl[...]) + dot(rl[at, :], dh[...])
        row = lax.broadcasted_iota(I32, (TILE, SPLITS), 0) + i * TILE
        return tuple(
            carry[l] + jnp.sum(jnp.where(row == index, value[:, l * SPLITS : (l + 1) * SPLITS], 0.0), axis=0, keepdims=True)
            for l, index in enumerate((splits[0], a1, a2))
        )

    along = lax.fori_loop(0, KIDS // TILE, root_body, (jnp.zeros((1, SPLITS), F32),) * LEVELS)

    scale = 0.5 / float(WIDTH) ** 0.5

    def level(l, offset, chains):
        zero = jnp.zeros((1, SPLITS), F32)
        chains = [(cluster.astype(F32), odd, seed_row, ahead) for cluster, odd, seed_row, ahead in chains]
        own = splits[l].astype(F32)

        def body(i, carry):
            at = pl.ds(aligned(i * TILE, TILE), TILE)
            member = memc[at, l : l + 1]
            squares = sq[at, :]
            hit = member == own
            value = proj[at, l * SPLITS : (l + 1) * SPLITS] + offset
            gap = jnp.sum(jnp.where(hit, value, 0.0), axis=1, keepdims=True)
            inside = jnp.sum(jnp.where(hit, 1.0, 0.0), axis=1, keepdims=True)
            first = lax.logistic(gap * scale)
            second = 1.0 - first
            cwbuf[at, l : l + 1] = first * inside
            out = []
            for j, part in enumerate((first, second)):
                weight = jnp.where(hit, part, 0.0)
                high, low = two(weight)
                w_hi[at, j * SPLITS : (j + 1) * SPLITS] = high
                w_lo[at, j * SPLITS : (j + 1) * SPLITS] = low
                out.append(jnp.sum(weight, axis=0, keepdims=True))
                out.append(jnp.sum(weight * squares, axis=0, keepdims=True))
            row = lax.broadcasted_iota(I32, (TILE, SPLITS), 0) + i * TILE
            for cluster, odd, seed_row, ahead in chains:
                weight = jnp.where(member == cluster, jnp.where(odd, second, first), 0.0)
                both = weight + jnp.where(row == seed_row, 0.5, 0.0)
                out.append(jnp.sum(both * proj[at, ahead * SPLITS : (ahead + 1) * SPLITS], axis=0, keepdims=True))
                out.append(jnp.sum(weight, axis=0, keepdims=True))
            return tuple(a + b for a, b in zip(carry, out))

        return list(lax.fori_loop(0, tiles, body, (zero,) * (4 + 2 * len(chains))))

    def add_up(dst, q):
        at = slice(256 * q, 256 * q + 256)
        wide = w_hi[:, :KIDS]
        dst[at, :] = dot(eth[at, :], wide) + dot(etl[at, :], wide) + dot(eth[at, :], w_lo[...])

    offset = -0.5 * along[0] - 0.25 * norm[0:1, :]
    got0 = level(0, offset, [(a1, odd1, seed1, 1), (a2, odd20, seed20, 2)])
    sums[1].start(got0)
    add_up(x0, 0)
    add_up(x0, 1)
    sums[1].middle()
    rs_u.start_two()
    add_up(x0, 2)
    for q in range(PARTS):
        rs_0.start_core(q)
    got0 = sums[1].finish()

    rs_0.start_one()
    parent = (got0[4:5, :] + 0.5 * along[1]) / (got0[5:6, :] + 1.0)
    offset = -0.5 * parent - 0.25 * norm[1:2, :]
    got1 = level(1, offset, [(mid2, odd2, seed2, 2)])
    sums[2].start(got1)
    add_up(x1, 0)
    add_up(x1, 1)
    sums[2].middle()
    rs_u.start_three()
    rs_0.start_two()
    add_up(x1, 2)
    for q in range(PARTS):
        rs_1.start_core(q)
    got1 = sums[2].finish()

    rs_1.start_one()
    older = (got0[6:7, :] + 0.5 * along[2]) / (got0[7:8, :] + 1.0)
    parent = (got1[4:5, :] + 0.5 * older) / (got1[5:6, :] + 1.0)
    offset = -0.5 * parent - 0.25 * norm[2:3, :]
    got2 = level(2, offset, [])
    sums[3].start(got2)
    for q in range(PARTS):
        add_up(x2, q)
        rs_2.start_core(q)
    sums[3].middle()
    rs_2.start_one()
    rs_0.start_three()
    rs_1.start_two()
    cw_ref[...] = jnp.transpose(cwbuf[...])[0:LEVELS]
    own_u = rs_u.finish_all()
    rs_2.start_two()
    rs_1.start_three()

    def flat(kid):
        return (kid & 1) * SPLITS + (kid >> 1)

    def seeds_of(l, parent):
        up = own_u[:, l * SPLITS : (l + 1) * SPLITS]
        diff = own_d[:, l * SPLITS : (l + 1) * SPLITS]
        return 0.5 * jnp.concatenate([parent + 0.5 * (up + diff), parent + 0.5 * (up - diff)], axis=1)

    def parents(from_, kid):
        line = lax.broadcasted_iota(I32, (KIDS, SPLITS), 0)
        return jnp.dot(from_, jnp.where(line == kid, 1.0, 0.0).astype(F32), precision=HIGH, preferred_element_type=F32)

    def counts_of(got):
        return jnp.concatenate([got[0:1, :], got[2:3, :]], axis=1)

    def error_of(count, centre, mine):
        return 0.25 * jnp.sum(count * centre * centre - 2.0 * centre * mine, axis=0, keepdims=True)

    roots = jnp.concatenate([roott[pl.ds(aligned(own_row(links, q), 8), 8), :] for q in range(PARTS)], axis=0)
    n0, n1 = counts_of(got0), counts_of(got1)
    own_0 = rs_0.finish_all()
    c1 = (own_0 + seeds_of(0, parents(roots, splits[0]))) / (n0 + 1.0)
    err0 = error_of(n0, c1, own_0)
    got2 = sums[3].finish()
    n2 = counts_of(got2)
    rs_2.start_three()
    own_1 = rs_1.finish_all()
    c2 = (own_1 + seeds_of(1, parents(c1, flat(kid1)))) / (n1 + 1.0)
    err1 = error_of(n1, c2, own_1)
    seeds2 = seeds_of(2, parents(c2, flat(kid2)))
    part, err2 = [], 0.0
    for q in range(PARTS):
        mine = rs_2.finish(q)
        centre = (mine + seeds2[8 * q : 8 * q + 8]) / (n2 + 1.0)
        ag_c.start_two(q, centre)
        err2 = err2 + error_of(n2, centre, mine)
    sums[4].start([e[:, j * SPLITS : (j + 1) * SPLITS] for e in (err0, err1, err2) for j in range(2)])
    ag_c.start_one()
    sums[4].middle()
    ag_c.start_core()

    copies = []

    def weave(q, half):
        w = 2 * q + half
        rows = cf[pl.ds(aligned(TILE * w, TILE), TILE), :]
        for j in range(2):
            woven[w, pl.ds(j, SPLITS, stride=2), :] = jnp.transpose(rows[:, j * SPLITS : (j + 1) * SPLITS])
        copy = pltpu.make_async_copy(
            woven.at[w], cent_hbm.at[:, pl.ds(aligned(w * TILE, TILE), TILE)], sem_out.at[len(copies)]
        )
        copy.start()
        copies.append(copy)

    c = me["c"]
    for q in range(PARTS):
        weave(q, c)
    total = sums[4].finish()
    lines = []
    for l, (got, n) in enumerate(((got0, n0), (got1, n1), (got2, n2))):
        energy = jnp.concatenate([got[1:2, :], got[3:4, :]], axis=1)
        error = jnp.concatenate([total[2 * l : 2 * l + 1, :], total[2 * l + 1 : 2 * l + 2, :]], axis=1)
        lines.append((energy + error) / ((n + 1.0) * WIDTH))
    lines.append(jnp.zeros((8 - LEVELS, KIDS), F32))
    line = lax.broadcasted_iota(I32, (KIDS, KIDS), 0)
    kid = lax.broadcasted_iota(I32, (KIDS, KIDS), 1)
    order = jnp.where(line == flat(kid), 1.0, 0.0).astype(F32)
    spread_ref[...] = jnp.dot(
        jnp.concatenate(lines, axis=0), order, precision=HIGH, preferred_element_type=F32
    )[0:LEVELS]
    for q in range(PARTS):
        ag_c.wait(q)
        weave(q, 1 - c)
    for copy in copies:
        copy.wait()
    links.drain()


def scratch_shapes():
    vm = pltpu.VMEM
    widths = (WIDTH, WIDTH, KIDS, KIDS, KIDS)
    shapes = [
        vm((ROWS, WIDTH), F32), vm((KIDS, WIDTH), F32),
        vm((ROWS, WIDTH), BF), vm((ROWS, WIDTH), BF), vm((WIDTH, ROWS), BF), vm((WIDTH, ROWS), BF),
        vm((KIDS, WIDTH), BF), vm((KIDS, WIDTH), BF), vm((WIDTH, KIDS), F32),
        vm((ROWS, WIDTH), BF), vm((ROWS, KIDS), BF),
        vm((WIDTH, WIDTH), BF), vm((WIDTH, WIDTH), BF), vm((ROWS, WIDTH), F32),
        vm((ROWS, 1), F32), vm((ROWS, TILE), F32), vm((SPLITS, TILE), F32), vm((ROWS, TILE), F32),
    ]
    shapes += [vm((WIDTH, n), F32) for n in widths]
    shapes += [vm((WIDTH, WIDTH), F32), vm((WIDTH, KIDS), F32)]
    shapes += [vm((PARTS, 128, n), F32) for n in widths]
    shapes += [vm((PARTS, 3, 32, n), F32) for n in widths]
    shapes += [vm((PARTS, 3, 8, n), F32) for n in widths]
    shapes += [vm((PARTS, 4, 8, n), F32) for n in widths]
    dma = pltpu.SemaphoreType.DMA
    shapes += [vm((5, 8, 8, SPLITS), F32), vm((5, 16, 8, SPLITS), F32)]
    shapes += [vm((WIDTH // TILE, KIDS, TILE), F32)]
    shapes += [dma((5, 2, PARTS, 10)), dma((2, 2, PARTS, 7)), dma((5, 2, 22)), dma((ROWS // TILE + 1,)), dma((6,))]
    return shapes


def on_device(embeddings, root_centroids, member_ids, split_order, seed_rows):
    vmem = pl.BlockSpec(memory_space=pltpu.VMEM)
    hbm = pl.BlockSpec(memory_space=pl.ANY)
    return pl.pallas_call(
        kernel,
        out_shape=(
            jax.ShapeDtypeStruct((KIDS, WIDTH), F32),
            jax.ShapeDtypeStruct((LEVELS, KIDS), F32),
            jax.ShapeDtypeStruct((LEVELS, ROWS), F32),
        ),
        in_specs=[hbm, hbm, vmem, vmem, vmem],
        out_specs=(hbm, vmem, vmem),
        scratch_shapes=scratch_shapes(),
        compiler_params=pltpu.CompilerParams(
            collective_id=0, has_side_effects=True, vmem_limit_bytes=66_000_000
        ),
    )(embeddings, root_centroids, member_ids, split_order, seed_rows.transpose(0, 2, 1))


def solution(mesh):
    split = Mesh(mesh.devices.reshape(4, 4, 2, 4), AXES)
    everywhere = ("z", "y", "c", "x")
    in_specs = (P(everywhere, None), P(), P(None, everywhere), P(), P())
    out_specs = (P(), P(), P(None, everywhere))
    return jax.shard_map(on_device, mesh=split, in_specs=in_specs, out_specs=out_specs, check_vma=False)
```

```python
import jax
import jax.numpy as jnp
from jax import lax
from jax.experimental import pallas as pl
from jax.experimental.pallas import tpu as pltpu
from jax.sharding import Mesh
from jax.sharding import PartitionSpec as P

F32 = jnp.float32
BF = jnp.bfloat16
I32 = jnp.int32
MESH = pl.DeviceIdType.MESH
HIGH = lax.Precision.HIGHEST

AXES = ("z", "y", "c", "x")
SIZE = {"z": 4, "y": 4, "c": 2, "x": 4}
ORDERS = (("x", "y", "z"), ("y", "z", "x"), ("z", "x", "y"))
PARTS = 3
ROWS = 1024
WIDTH = 768
SPLITS = 256
LEVELS = 3
FAR_FIRST = (2, 1, 3)
KIDS = 512
TILE = 128


def two(value):
    high = value.astype(BF)
    return high, (value - high.astype(F32)).astype(BF)


def dot(a, b):
    return jnp.dot(a, b, preferred_element_type=F32)


def aligned(value, step):
    return pl.multiple_of(value, step)


class Links:
    def __init__(self):
        self.me = {a: lax.axis_index(a) for a in AXES}
        self.started = []

    def at(self, axis, step):
        return lax.rem(self.me[axis] + step, SIZE[axis])

    def send(self, src, dst, send_sem, recv_sem, device):
        copy = pltpu.make_async_remote_copy(
            src_ref=src, dst_ref=dst, send_sem=send_sem, recv_sem=recv_sem, device_id=device, device_id_type=MESH
        )
        copy.start()
        self.started.append(copy)
        return copy

    def drain(self):
        for copy in self.started:
            copy.wait_send()
        self.started = []


def near_group(links):
    return [{"x": links.at("x", i), "c": links.at("c", j)} for i in range(4) for j in range(2) if i or j]


def far_group(links):
    return [{"z": links.at("z", i), "y": links.at("y", j)} for i in range(4) for j in range(4) if i or j]


class AllSum:
    def __init__(self, links, near, far, sems):
        self.links, self.near, self.far, self.sems = links, near, far, sems

    def start(self, rows):
        links = self.links
        slot = links.me["x"] * 2 + links.me["c"]
        for i, row in enumerate(rows):
            self.near[slot, i : i + 1, :] = row
        if len(rows) < 8:
            self.near[slot, len(rows) :, :] = jnp.zeros((8 - len(rows), SPLITS), F32)
        mine = self.near.at[slot]
        self.waits = [
            links.send(mine, mine, self.sems.at[0, k], self.sems.at[1, k], device)
            for k, device in enumerate(near_group(links))
        ]

    def middle(self):
        links = self.links
        for copy in self.waits:
            copy.wait_recv()
        total = self.near[0]
        for k in range(1, 8):
            total = total + self.near[k]
        slot = links.me["z"] * 4 + links.me["y"]
        self.far[slot] = total
        mine = self.far.at[slot]
        self.waits = [
            links.send(mine, mine, self.sems.at[0, 7 + k], self.sems.at[1, 7 + k], device)
            for k, device in enumerate(far_group(links))
        ]

    def finish(self):
        for copy in self.waits:
            copy.wait_recv()
        total = self.far[0]
        for k in range(1, 16):
            total = total + self.far[k]
        return total


def add_into(dst, first, rows, sources, step):
    @pl.loop(0, rows // step)
    def _(i):
        at = pl.ds(aligned(first + i * step, step), step)
        total = dst[at, :]
        for source in sources:
            total = total + source[pl.ds(aligned(i * step, step), step), :]
        dst[at, :] = total


class Scatter:
    def __init__(self, links, data, core, one, two_, three, sems):
        self.links, self.data, self.sems = links, data, sems
        self.core, self.one, self.two, self.three = core, one, two_, three
        self.waits = [[] for _ in range(PARTS)]

    def send(self, q, k, src, dst, device):
        self.waits[q].append(self.links.send(src, dst, self.sems.at[0, q, k], self.sems.at[1, q, k], device))

    def wait(self, q):
        for copy in self.waits[q]:
            copy.wait_recv()
        self.waits[q] = []

    def start_core(self, q):
        other = 1 - self.links.me["c"]
        src = self.data.at[pl.ds(aligned(256 * q + 128 * other, 128), 128), :]
        self.send(q, 0, src, self.core.at[q], {"c": other})

    def start_one(self, q):
        links = self.links
        self.wait(q)
        base = 256 * q + 128 * links.me["c"]
        add_into(self.data, base, 128, [self.core.at[q]], 16)
        axis = ORDERS[q][0]
        for k in FAR_FIRST:
            other = links.at(axis, k)
            src = self.data.at[pl.ds(aligned(base + 32 * other, 32), 32), :]
            self.send(q, k, src, self.one.at[q, k - 1], {axis: other})

    def start_two(self, q):
        links = self.links
        self.wait(q)
        base = 256 * q + 128 * links.me["c"] + 32 * links.me[ORDERS[q][0]]
        add_into(self.data, base, 32, [self.one.at[q, k] for k in range(3)], 8)
        axis = ORDERS[q][1]
        for k in FAR_FIRST:
            other = links.at(axis, k)
            src = self.data.at[pl.ds(aligned(base + 8 * other, 8), 8), :]
            self.send(q, 3 + k, src, self.two.at[q, k - 1], {axis: other})

    def start_three(self, q):
        links = self.links
        self.wait(q)
        base = own_row(links, q)
        axis = ORDERS[q][2]
        slot = links.me[axis]
        total = self.data[pl.ds(aligned(base, 8), 8), :]
        for k in range(3):
            total = total + self.two[q, k]
        self.three[q, slot] = total
        mine = self.three.at[q, slot]
        for k in FAR_FIRST:
            self.send(q, 6 + k, mine, mine, {axis: links.at(axis, k)})

    def every(self, step):
        for q in range(PARTS):
            step(q)

    def finish(self, q):
        self.wait(q)
        return ((self.three[q, 0] + self.three[q, 1]) + self.three[q, 2]) + self.three[q, 3]

    def finish_all(self):
        return jnp.concatenate([self.finish(q) for q in range(PARTS)], axis=0)


def own_row(links, q):
    first, second, _ = ORDERS[q]
    return 256 * q + 128 * links.me["c"] + 32 * links.me[first] + 8 * links.me[second]


class Gather:
    def __init__(self, links, data, sems):
        self.links, self.data, self.sems = links, data, sems
        self.waits = [[] for _ in range(PARTS)]

    def push(self, q, k, base, rows, device):
        block = self.data.at[pl.ds(aligned(base, rows), rows), :]
        self.waits[q].append(self.links.send(block, block, self.sems.at[0, q, k], self.sems.at[1, q, k], device))

    def wait(self, q):
        for copy in self.waits[q]:
            copy.wait_recv()
        self.waits[q] = []

    def start_two(self, q, own):
        links = self.links
        base = own_row(links, q)
        self.data[pl.ds(aligned(base, 8), 8), :] = own
        axis = ORDERS[q][1]
        for k in FAR_FIRST:
            self.push(q, k, base, 8, {axis: links.at(axis, k)})

    def start_one(self):
        links = self.links
        for q in range(PARTS):
            self.wait(q)
            base = 256 * q + 128 * links.me["c"] + 32 * links.me[ORDERS[q][0]]
            axis = ORDERS[q][0]
            for k in FAR_FIRST:
                self.push(q, 3 + k, base, 32, {axis: links.at(axis, k)})

    def start_core(self):
        c = self.links.me["c"]
        for q in range(PARTS):
            self.wait(q)
            self.push(q, 0, 256 * q + 128 * c, 128, {"c": 1 - c})


def pick(index, columns):
    hit = lax.broadcasted_iota(I32, (SPLITS, SPLITS), 0) == index
    return [jnp.sum(jnp.where(hit, column, 0.0), axis=0, keepdims=True).astype(I32) for column in columns]


def kernel(e_hbm, root_hbm, mem_ref, split_ref, seed_ref, cent_hbm, spread_ref, cw_ref, *scratch):
    (
        e_ref, root_ref,
        eh, el, eth, etl, rh, rl, roott, oh, w_lo, dh, dl, proj, sq, memc, colt, cwbuf, firsts,
        xd, xu, x0, x1, x2, df, cf,
        core_d, core_u, core_0, core_1, core_2,
        one_d, one_u, one_0, one_1, one_2,
        two_d, two_u, two_0, two_1, two_2,
        three_d, three_u, three_0, three_1, three_2,
        near, far, woven, sem_rs, sem_ag, sem_ar, sem_in, sem_out,
    ) = scratch
    w_hi = oh
    links = Links()
    me = links.me
    barrier = pltpu.get_barrier_semaphore()
    peers = near_group(links) + far_group(links)
    for device in peers:
        pl.semaphore_signal(barrier, inc=1, device_id=device, device_id_type=MESH)

    tiles = ROWS // TILE

    def fetch(i):
        at = pl.ds(aligned(i * TILE, TILE), TILE)
        return pltpu.make_async_copy(e_hbm.at[at, :], e_ref.at[at, :], sem_in.at[i])

    root_copy = pltpu.make_async_copy(root_hbm, root_ref, sem_in.at[tiles])
    for i in range(tiles):
        fetch(i).start()
    root_copy.start()

    rs_d = Scatter(links, xd, core_d, one_d, two_d, three_d, sem_rs.at[0])
    rs_u = Scatter(links, xu, core_u, one_u, two_u, three_u, sem_rs.at[1])
    rs_0 = Scatter(links, x0, core_0, one_0, two_0, three_0, sem_rs.at[2])
    rs_1 = Scatter(links, x1, core_1, one_1, two_1, three_1, sem_rs.at[3])
    rs_2 = Scatter(links, x2, core_2, one_2, two_2, three_2, sem_rs.at[4])
    ag_d = Gather(links, df, sem_ag.at[0])
    ag_c = Gather(links, cf, sem_ag.at[1])
    sums = [AllSum(links, near.at[i], far.at[i], sem_ar.at[i]) for i in range(5)]

    first_row = (me["z"] * 32 + me["y"] * 8 + me["c"] * 4 + me["x"]) * ROWS
    splits = [split_ref[l : l + 1, :SPLITS] for l in range(LEVELS)]
    seed = [[seed_ref[l, j : j + 1, :] - first_row for j in range(2)] for l in range(LEVELS)]

    def place(sign):
        @pl.loop(0, tiles)
        def _(i):
            at = pl.ds(aligned(i * TILE, TILE), TILE)
            row = lax.broadcasted_iota(I32, (TILE, SPLITS), 0) + i * TILE
            for l in range(LEVELS):
                value = jnp.where(row == seed[l][0], 1.0, 0.0) + jnp.where(row == seed[l][1], sign, 0.0)
                oh[at, l * SPLITS : (l + 1) * SPLITS] = value.astype(BF)

    place(-1.0)

    @pl.loop(0, tiles)
    def _(i):
        fetch(i).wait()
        at = pl.ds(aligned(i * TILE, TILE), TILE)
        high, low = two(jnp.transpose(e_ref[at, :]))
        eth[:, at] = high
        etl[:, at] = low

    def as_they_lie(i, carry):
        at = pl.ds(aligned(i * TILE, TILE), TILE)
        rows = e_ref[at, :]
        high, low = two(rows)
        eh[at, :] = high
        el[at, :] = low
        squares = jnp.sum(rows * rows, axis=1, keepdims=True)
        sq[at, :] = squares
        return tuple(
            carry[l] + jnp.sum(oh[at, l * SPLITS : (l + 1) * SPLITS].astype(F32) * squares, axis=0, keepdims=True)
            for l in range(LEVELS)
        )

    def select_rows(dst, q):
        at = slice(256 * q, 256 * q + 256)
        dst[at, :] = dot(eth[at, :], oh[...]) + dot(etl[at, :], oh[...])

    select_rows(xd, 0)
    pl.semaphore_wait(barrier, len(peers))
    rs_d.start_core(0)
    select_rows(xd, 1)
    rs_d.start_core(1)
    select_rows(xd, 2)
    rs_d.start_core(2)
    rs_d.start_one(0)

    lines = [splits[0], splits[1], seed_ref[0, 0:1, :], seed_ref[0, 1:2, :], seed_ref[1, 0:1, :], seed_ref[1, 1:2, :]]
    lines = [line.astype(F32) for line in lines] + [jnp.zeros((TILE - 6, SPLITS), F32)]
    colt[...] = jnp.transpose(jnp.concatenate(lines, axis=0))
    memc[...] = jnp.transpose(
        jnp.concatenate([mem_ref[...].astype(F32), jnp.zeros((TILE - LEVELS, ROWS), F32)], axis=0)
    )
    col = [colt[:, k : k + 1] for k in range(6)]
    kid1 = splits[1]
    a1, s10, s11 = pick(kid1 >> 1, [col[0], col[2], col[3]])
    odd1 = (kid1 & 1) == 1
    seed1 = jnp.where(odd1, s11, s10) - first_row
    kid2 = splits[2]
    mid2, s20, s21 = pick(kid2 >> 1, [col[1], col[4], col[5]])
    odd2 = (kid2 & 1) == 1
    seed2 = jnp.where(odd2, s21, s20) - first_row
    a2, t20, t21 = pick(mid2 >> 1, [col[0], col[2], col[3]])
    odd20 = (mid2 & 1) == 1
    seed20 = jnp.where(odd20, t21, t20) - first_row
    rs_d.start_one(1)
    rs_d.start_one(2)
    norms = lax.fori_loop(0, tiles, as_they_lie, (jnp.zeros((1, SPLITS), F32),) * LEVELS)
    sums[0].start(list(norms))

    root_copy.wait()

    @pl.loop(0, KIDS // TILE)
    def _(i):
        at = pl.ds(aligned(i * TILE, TILE), TILE)
        rows = root_ref[at, :]
        high, low = two(rows)
        rh[at, :] = high
        rl[at, :] = low
        roott[:, at] = jnp.transpose(rows)

    place(1.0)
    sums[0].middle()
    rs_d.every(rs_d.start_two)
    select_rows(xu, 0)
    rs_d.every(rs_d.start_three)
    select_rows(xu, 1)
    own_d = []
    for q in range(PARTS):
        own_d.append(rs_d.finish(q))
        ag_d.start_two(q, own_d[q])
    own_d = jnp.concatenate(own_d, axis=0)
    select_rows(xu, 2)
    ag_d.start_one()
    norm = sums[0].finish()
    ag_d.start_core()
    for q in range(PARTS):
        rs_u.start_core(q)

    for q in range(PARTS):
        ag_d.wait(q)
        for i in range(2):
            at = slice(256 * q + 128 * i, 256 * q + 128 * (i + 1))
            high, low = two(df[at, :])
            dh[at, :] = high
            dl[at, :] = low

    def products(first):
        @pl.loop(first, first + 2)
        def _(i):
            at = pl.ds(aligned(i * 256, 256), 256)
            proj[at, :] = dot(eh[at, :], dh[...]) + dot(eh[at, :], dl[...]) + dot(el[at, :], dh[...])

    products(0)
    rs_u.every(rs_u.start_one)
    products(2)

    def root_products(levels, indices):
        cols = slice(levels[0] * SPLITS, (levels[-1] + 1) * SPLITS)

        def body(i, carry):
            at = pl.ds(aligned(i * TILE, TILE), TILE)
            value = dot(rh[at, :], dh[:, cols]) + dot(rh[at, :], dl[:, cols]) + dot(rl[at, :], dh[:, cols])
            row = lax.broadcasted_iota(I32, (TILE, SPLITS), 0) + i * TILE
            return tuple(
                carry[k] + jnp.sum(jnp.where(row == index, value[:, k * SPLITS : (k + 1) * SPLITS], 0.0), axis=0, keepdims=True)
                for k, index in enumerate(indices)
            )

        return lax.fori_loop(0, KIDS // TILE, body, (jnp.zeros((1, SPLITS), F32),) * len(levels))

    along0 = root_products([0], [splits[0]])[0]

    scale = 0.5 / float(WIDTH) ** 0.5

    def level(l, offset, chains):
        zero = jnp.zeros((1, SPLITS), F32)
        chains = [(cluster.astype(F32), odd, seed_row, ahead) for cluster, odd, seed_row, ahead in chains]
        own = splits[l].astype(F32)

        def body(i, carry):
            at = pl.ds(aligned(i * TILE, TILE), TILE)
            member = memc[at, l : l + 1]
            value = proj[at, l * SPLITS : (l + 1) * SPLITS] + offset
            gap = jnp.sum(jnp.where(member == own, value, 0.0), axis=1, keepdims=True)
            first = lax.logistic(gap * scale)
            second = 1.0 - first
            firsts[at, :] = first
            out = []
            row = lax.broadcasted_iota(I32, (TILE, SPLITS), 0) + i * TILE
            for cluster, odd, seed_row, ahead in chains:
                weight = jnp.where(member == cluster, jnp.where(odd, second, first), 0.0)
                both = weight + jnp.where(row == seed_row, 0.5, 0.0)
                out.append(jnp.sum(both * proj[at, ahead * SPLITS : (ahead + 1) * SPLITS], axis=0, keepdims=True))
                out.append(jnp.sum(weight, axis=0, keepdims=True))
            return tuple(a + b for a, b in zip(carry, out))

        return list(lax.fori_loop(0, tiles, body, (zero,) * (2 * len(chains))))

    def weigh(l):
        zero = jnp.zeros((1, SPLITS), F32)
        own = splits[l].astype(F32)

        def body(i, carry):
            at = pl.ds(aligned(i * TILE, TILE), TILE)
            hit = memc[at, l : l + 1] == own
            first = firsts[at, :]
            squares = sq[at, :]
            inside = jnp.sum(jnp.where(hit, 1.0, 0.0), axis=1, keepdims=True)
            cwbuf[at, l : l + 1] = first * inside
            out = []
            for j, part in enumerate((first, 1.0 - first)):
                weight = jnp.where(hit, part, 0.0)
                high, low = two(weight)
                w_hi[at, j * SPLITS : (j + 1) * SPLITS] = high
                w_lo[at, j * SPLITS : (j + 1) * SPLITS] = low
                out.append(jnp.sum(weight, axis=0, keepdims=True))
                out.append(jnp.sum(weight * squares, axis=0, keepdims=True))
            return tuple(a + b for a, b in zip(carry, out))

        return list(lax.fori_loop(0, tiles, body, (zero,) * 4))

    def add_up(dst, q, j):
        at, cols = slice(256 * q, 256 * q + 256), slice(SPLITS * j, SPLITS * j + SPLITS)
        high = w_hi[:, cols]
        dst[at, cols] = dot(eth[at, :], high) + dot(etl[at, :], high) + dot(eth[at, :], w_lo[:, cols])

    offset = -0.5 * along0 - 0.25 * norm[0:1, :]
    got0 = level(0, offset, [(a1, odd1, seed1, 1), (a2, odd20, seed20, 2)])
    sums[1].start(got0)
    tally0 = weigh(0)
    add_up(x0, 0, 0)
    sums[1].middle()
    along1, along2 = root_products([1, 2], [a1, a2])
    add_up(x0, 0, 1)
    rs_0.start_core(0)
    for q in (1, 2):
        for j in (0, 1):
            add_up(x0, q, j)
        rs_0.start_core(q)
    got0 = sums[1].finish()

    parent = (got0[0:1, :] + 0.5 * along1) / (got0[1:2, :] + 1.0)
    offset = -0.5 * parent - 0.25 * norm[1:2, :]
    got1 = level(1, offset, [(mid2, odd2, seed2, 2)])
    sums[2].start(got1 + tally0)
    tally1 = weigh(1)
    rs_u.every(rs_u.start_two)
    add_up(x1, 0, 0)
    sums[2].middle()
    add_up(x1, 0, 1)
    rs_1.start_core(0)
    add_up(x1, 1, 0)
    rs_0.every(rs_0.start_one)
    add_up(x1, 1, 1)
    rs_1.start_core(1)
    add_up(x1, 2, 0)
    add_up(x1, 2, 1)
    rs_1.start_core(2)
    got1 = sums[2].finish()

    rs_1.every(rs_1.start_one)
    older = (got0[2:3, :] + 0.5 * along2) / (got0[3:4, :] + 1.0)
    parent = (got1[0:1, :] + 0.5 * older) / (got1[1:2, :] + 1.0)
    offset = -0.5 * parent - 0.25 * norm[2:3, :]
    level(2, offset, [])
    tally2 = weigh(2)
    sums[3].start(tally1 + tally2)
    for q in range(PARTS):
        for j in (0, 1):
            add_up(x2, q, j)
        rs_2.start_core(q)
        if q:
            rs_2.start_one(q - 1)
    rs_2.start_one(2)
    sums[3].middle()
    rs_u.every(rs_u.start_three)
    rs_0.every(rs_0.start_two)
    rs_1.every(rs_1.start_two)
    cw_ref[...] = jnp.transpose(cwbuf[...])[0:LEVELS]
    own_u = rs_u.finish_all()
    rs_2.every(rs_2.start_two)
    rs_0.every(rs_0.start_three)
    rs_1.every(rs_1.start_three)

    def flat(kid):
        return (kid & 1) * SPLITS + (kid >> 1)

    def seeds_of(l, parent):
        up = own_u[:, l * SPLITS : (l + 1) * SPLITS]
        diff = own_d[:, l * SPLITS : (l + 1) * SPLITS]
        return 0.5 * jnp.concatenate([parent + 0.5 * (up + diff), parent + 0.5 * (up - diff)], axis=1)

    def parents(from_, kid):
        line = lax.broadcasted_iota(I32, (KIDS, SPLITS), 0)
        return jnp.dot(from_, jnp.where(line == kid, 1.0, 0.0).astype(F32), precision=HIGH, preferred_element_type=F32)

    def counts_of(got):
        return jnp.concatenate([got[0:1, :], got[2:3, :]], axis=1)

    def error_of(count, centre, mine):
        return 0.25 * jnp.sum(count * centre * centre - 2.0 * centre * mine, axis=0, keepdims=True)

    roots = jnp.concatenate([roott[pl.ds(aligned(own_row(links, q), 8), 8), :] for q in range(PARTS)], axis=0)
    got0 = got1[2:6, :]
    n0 = counts_of(got0)
    own_0 = rs_0.finish_all()
    c1 = (own_0 + seeds_of(0, parents(roots, splits[0]))) / (n0 + 1.0)
    err0 = error_of(n0, c1, own_0)
    got2 = sums[3].finish()
    got1, got2 = got2[0:4, :], got2[4:8, :]
    n1, n2 = counts_of(got1), counts_of(got2)
    rs_2.every(rs_2.start_three)
    own_1 = rs_1.finish_all()
    c2 = (own_1 + seeds_of(1, parents(c1, flat(kid1)))) / (n1 + 1.0)
    err1 = error_of(n1, c2, own_1)
    seeds2 = seeds_of(2, parents(c2, flat(kid2)))
    part, err2 = [], 0.0
    for q in range(PARTS):
        mine = rs_2.finish(q)
        centre = (mine + seeds2[8 * q : 8 * q + 8]) / (n2 + 1.0)
        ag_c.start_two(q, centre)
        err2 = err2 + error_of(n2, centre, mine)
    sums[4].start([e[:, j * SPLITS : (j + 1) * SPLITS] for e in (err0, err1, err2) for j in range(2)])
    ag_c.start_one()
    sums[4].middle()
    ag_c.start_core()

    copies = []

    def weave(q, half):
        w = 2 * q + half
        rows = cf[pl.ds(aligned(TILE * w, TILE), TILE), :]
        for j in range(2):
            woven[w, pl.ds(j, SPLITS, stride=2), :] = jnp.transpose(rows[:, j * SPLITS : (j + 1) * SPLITS])
        copy = pltpu.make_async_copy(
            woven.at[w], cent_hbm.at[:, pl.ds(aligned(w * TILE, TILE), TILE)], sem_out.at[len(copies)]
        )
        copy.start()
        copies.append(copy)

    c = me["c"]
    for q in range(PARTS):
        weave(q, c)
    total = sums[4].finish()
    lines = []
    for l, (got, n) in enumerate(((got0, n0), (got1, n1), (got2, n2))):
        energy = jnp.concatenate([got[1:2, :], got[3:4, :]], axis=1)
        error = jnp.concatenate([total[2 * l : 2 * l + 1, :], total[2 * l + 1 : 2 * l + 2, :]], axis=1)
        lines.append((energy + error) / ((n + 1.0) * WIDTH))
    lines.append(jnp.zeros((8 - LEVELS, KIDS), F32))
    line = lax.broadcasted_iota(I32, (KIDS, KIDS), 0)
    kid = lax.broadcasted_iota(I32, (KIDS, KIDS), 1)
    order = jnp.where(line == flat(kid), 1.0, 0.0).astype(F32)
    spread_ref[...] = jnp.dot(
        jnp.concatenate(lines, axis=0), order, precision=HIGH, preferred_element_type=F32
    )[0:LEVELS]
    for q in range(PARTS):
        ag_c.wait(q)
        weave(q, 1 - c)
    for copy in copies:
        copy.wait()
    links.drain()


def scratch_shapes():
    vm = pltpu.VMEM
    widths = (WIDTH, WIDTH, KIDS, KIDS, KIDS)
    shapes = [
        vm((ROWS, WIDTH), F32), vm((KIDS, WIDTH), F32),
        vm((ROWS, WIDTH), BF), vm((ROWS, WIDTH), BF), vm((WIDTH, ROWS), BF), vm((WIDTH, ROWS), BF),
        vm((KIDS, WIDTH), BF), vm((KIDS, WIDTH), BF), vm((WIDTH, KIDS), F32),
        vm((ROWS, WIDTH), BF), vm((ROWS, KIDS), BF),
        vm((WIDTH, WIDTH), BF), vm((WIDTH, WIDTH), BF), vm((ROWS, WIDTH), F32),
        vm((ROWS, 1), F32), vm((ROWS, TILE), F32), vm((SPLITS, TILE), F32), vm((ROWS, TILE), F32), vm((ROWS, 1), F32),
    ]
    shapes += [vm((WIDTH, n), F32) for n in widths]
    shapes += [vm((WIDTH, WIDTH), F32), vm((WIDTH, KIDS), F32)]
    shapes += [vm((PARTS, 128, n), F32) for n in widths]
    shapes += [vm((PARTS, 3, 32, n), F32) for n in widths]
    shapes += [vm((PARTS, 3, 8, n), F32) for n in widths]
    shapes += [vm((PARTS, 4, 8, n), F32) for n in widths]
    dma = pltpu.SemaphoreType.DMA
    shapes += [vm((5, 8, 8, SPLITS), F32), vm((5, 16, 8, SPLITS), F32)]
    shapes += [vm((WIDTH // TILE, KIDS, TILE), F32)]
    shapes += [dma((5, 2, PARTS, 10)), dma((2, 2, PARTS, 7)), dma((5, 2, 22)), dma((ROWS // TILE + 1,)), dma((6,))]
    return shapes


def on_device(embeddings, root_centroids, member_ids, split_order, seed_rows):
    vmem = pl.BlockSpec(memory_space=pltpu.VMEM)
    hbm = pl.BlockSpec(memory_space=pl.ANY)
    return pl.pallas_call(
        kernel,
        out_shape=(
            jax.ShapeDtypeStruct((KIDS, WIDTH), F32),
            jax.ShapeDtypeStruct((LEVELS, KIDS), F32),
            jax.ShapeDtypeStruct((LEVELS, ROWS), F32),
        ),
        in_specs=[hbm, hbm, vmem, vmem, vmem],
        out_specs=(hbm, vmem, vmem),
        scratch_shapes=scratch_shapes(),
        compiler_params=pltpu.CompilerParams(
            collective_id=0, has_side_effects=True, vmem_limit_bytes=66_000_000
        ),
    )(embeddings, root_centroids, member_ids, split_order, seed_rows.transpose(0, 2, 1))


def solution(mesh):
    split = Mesh(mesh.devices.reshape(4, 4, 2, 4), AXES)
    everywhere = ("z", "y", "c", "x")
    in_specs = (P(everywhere, None), P(), P(None, everywhere), P(), P())
    out_specs = (P(), P(), P(None, everywhere))
    return jax.shard_map(on_device, mesh=split, in_specs=in_specs, out_specs=out_specs, check_vma=False)
```

```python
import jax
import jax.numpy as jnp
from jax import lax
from jax.experimental import pallas as pl
from jax.experimental.pallas import tpu as pltpu
from jax.sharding import Mesh
from jax.sharding import PartitionSpec as P

F32 = jnp.float32
BF = jnp.bfloat16
I32 = jnp.int32
MESH = pl.DeviceIdType.MESH
HIGH = lax.Precision.HIGHEST

AXES = ("z", "y", "c", "x")
SIZE = {"z": 4, "y": 4, "c": 2, "x": 4}
ORDERS = (("x", "y", "z"), ("y", "z", "x"), ("z", "x", "y"))
PARTS = 3
ROWS = 1024
WIDTH = 768
SPLITS = 256
LEVELS = 3
FAR_FIRST = (2, 1, 3)
KIDS = 512
TILE = 128


def two(value):
    high = value.astype(BF)
    return high, (value - high.astype(F32)).astype(BF)


def dot(a, b):
    return jnp.dot(a, b, preferred_element_type=F32)


def aligned(value, step):
    return pl.multiple_of(value, step)


class Links:
    def __init__(self):
        self.me = {a: lax.axis_index(a) for a in AXES}
        self.started = []

    def at(self, axis, step):
        return lax.rem(self.me[axis] + step, SIZE[axis])

    def send(self, src, dst, send_sem, recv_sem, device):
        copy = pltpu.make_async_remote_copy(
            src_ref=src, dst_ref=dst, send_sem=send_sem, recv_sem=recv_sem, device_id=device, device_id_type=MESH
        )
        copy.start()
        self.started.append(copy)
        return copy

    def drain(self):
        for copy in self.started:
            copy.wait_send()
        self.started = []


def near_group(links):
    return [{"x": links.at("x", i), "c": links.at("c", j)} for i in range(4) for j in range(2) if i or j]


def far_group(links):
    return [{"z": links.at("z", i), "y": links.at("y", j)} for i in range(4) for j in range(4) if i or j]


class AllSum:
    def __init__(self, links, near, far, sems):
        self.links, self.near, self.far, self.sems = links, near, far, sems

    def start(self, rows):
        links = self.links
        slot = links.me["x"] * 2 + links.me["c"]
        for i, row in enumerate(rows):
            self.near[slot, i : i + 1, :] = row
        if len(rows) < 8:
            self.near[slot, len(rows) :, :] = jnp.zeros((8 - len(rows), SPLITS), F32)
        mine = self.near.at[slot]
        self.waits = [
            links.send(mine, mine, self.sems.at[0, k], self.sems.at[1, k], device)
            for k, device in enumerate(near_group(links))
        ]

    def middle(self):
        links = self.links
        for copy in self.waits:
            copy.wait_recv()
        total = self.near[0]
        for k in range(1, 8):
            total = total + self.near[k]
        slot = links.me["z"] * 4 + links.me["y"]
        self.far[slot] = total
        mine = self.far.at[slot]
        self.waits = [
            links.send(mine, mine, self.sems.at[0, 7 + k], self.sems.at[1, 7 + k], device)
            for k, device in enumerate(far_group(links))
        ]

    def finish(self):
        for copy in self.waits:
            copy.wait_recv()
        total = self.far[0]
        for k in range(1, 16):
            total = total + self.far[k]
        return total


def add_into(dst, first, rows, sources, step):
    @pl.loop(0, rows // step)
    def _(i):
        at = pl.ds(aligned(first + i * step, step), step)
        total = dst[at, :]
        for source in sources:
            total = total + source[pl.ds(aligned(i * step, step), step), :]
        dst[at, :] = total


class Scatter:
    def __init__(self, links, data, core, one, two_, three, sems):
        self.links, self.data, self.sems = links, data, sems
        self.core, self.one, self.two, self.three = core, one, two_, three
        self.waits = [[] for _ in range(PARTS)]

    def send(self, q, k, src, dst, device):
        self.waits[q].append(self.links.send(src, dst, self.sems.at[0, q, k], self.sems.at[1, q, k], device))

    def wait(self, q):
        for copy in self.waits[q]:
            copy.wait_recv()
        self.waits[q] = []

    def start_core(self, q):
        other = 1 - self.links.me["c"]
        src = self.data.at[pl.ds(aligned(256 * q + 128 * other, 128), 128), :]
        self.send(q, 0, src, self.core.at[q], {"c": other})

    def start_one(self, q):
        links = self.links
        self.wait(q)
        base = 256 * q + 128 * links.me["c"]
        add_into(self.data, base, 128, [self.core.at[q]], 16)
        axis = ORDERS[q][0]
        for k in FAR_FIRST:
            other = links.at(axis, k)
            src = self.data.at[pl.ds(aligned(base + 32 * other, 32), 32), :]
            self.send(q, k, src, self.one.at[q, k - 1], {axis: other})

    def start_two(self, q):
        links = self.links
        self.wait(q)
        base = 256 * q + 128 * links.me["c"] + 32 * links.me[ORDERS[q][0]]
        add_into(self.data, base, 32, [self.one.at[q, k] for k in range(3)], 8)
        axis = ORDERS[q][1]
        for k in FAR_FIRST:
            other = links.at(axis, k)
            src = self.data.at[pl.ds(aligned(base + 8 * other, 8), 8), :]
            self.send(q, 3 + k, src, self.two.at[q, k - 1], {axis: other})

    def start_three(self, q):
        links = self.links
        self.wait(q)
        base = own_row(links, q)
        axis = ORDERS[q][2]
        slot = links.me[axis]
        total = self.data[pl.ds(aligned(base, 8), 8), :]
        for k in range(3):
            total = total + self.two[q, k]
        self.three[q, slot] = total
        mine = self.three.at[q, slot]
        for k in FAR_FIRST:
            self.send(q, 6 + k, mine, mine, {axis: links.at(axis, k)})

    def every(self, step):
        for q in range(PARTS):
            step(q)

    def finish(self, q):
        self.wait(q)
        return ((self.three[q, 0] + self.three[q, 1]) + self.three[q, 2]) + self.three[q, 3]

    def finish_all(self):
        return jnp.concatenate([self.finish(q) for q in range(PARTS)], axis=0)


def own_row(links, q):
    first, second, _ = ORDERS[q]
    return 256 * q + 128 * links.me["c"] + 32 * links.me[first] + 8 * links.me[second]


class Gather:
    def __init__(self, links, data, sems):
        self.links, self.data, self.sems = links, data, sems
        self.waits = [[] for _ in range(PARTS)]

    def push(self, q, k, base, rows, device):
        block = self.data.at[pl.ds(aligned(base, rows), rows), :]
        self.waits[q].append(self.links.send(block, block, self.sems.at[0, q, k], self.sems.at[1, q, k], device))

    def wait(self, q):
        for copy in self.waits[q]:
            copy.wait_recv()
        self.waits[q] = []

    def start_two(self, q, own):
        links = self.links
        base = own_row(links, q)
        self.data[pl.ds(aligned(base, 8), 8), :] = own
        axis = ORDERS[q][1]
        for k in FAR_FIRST:
            self.push(q, k, base, 8, {axis: links.at(axis, k)})

    def start_one(self):
        links = self.links
        for q in range(PARTS):
            self.wait(q)
            base = 256 * q + 128 * links.me["c"] + 32 * links.me[ORDERS[q][0]]
            axis = ORDERS[q][0]
            for k in FAR_FIRST:
                self.push(q, 3 + k, base, 32, {axis: links.at(axis, k)})

    def start_core(self):
        c = self.links.me["c"]
        for q in range(PARTS):
            self.wait(q)
            self.push(q, 0, 256 * q + 128 * c, 128, {"c": 1 - c})


def pick(index, columns):
    hit = lax.broadcasted_iota(I32, (SPLITS, SPLITS), 0) == index
    return [jnp.sum(jnp.where(hit, column, 0.0), axis=0, keepdims=True).astype(I32) for column in columns]


def kernel(e_hbm, root_hbm, mem_ref, split_ref, seed_ref, cent_hbm, spread_ref, cw_ref, *scratch):
    (
        e_ref, root_ref,
        eh, el, eth, etl, rh, rl, roott, oh, w_lo, dh, dl, proj, sq, memc, colt, cwbuf, firsts,
        xd, xu, x0, x1, x2, df, cf,
        core_d, core_u, core_0, core_1, core_2,
        one_d, one_u, one_0, one_1, one_2,
        two_d, two_u, two_0, two_1, two_2,
        three_d, three_u, three_0, three_1, three_2,
        near, far, woven, sem_rs, sem_ag, sem_ar, sem_in, sem_out,
    ) = scratch
    w_hi = oh
    links = Links()
    me = links.me
    barrier = pltpu.get_barrier_semaphore()
    peers = near_group(links) + far_group(links)
    for device in peers:
        pl.semaphore_signal(barrier, inc=1, device_id=device, device_id_type=MESH)

    tiles = ROWS // TILE

    def fetch(i):
        at = pl.ds(aligned(i * TILE, TILE), TILE)
        return pltpu.make_async_copy(e_hbm.at[at, :], e_ref.at[at, :], sem_in.at[i])

    root_copy = pltpu.make_async_copy(root_hbm, root_ref, sem_in.at[tiles])
    for i in range(tiles):
        fetch(i).start()
    root_copy.start()

    rs_d = Scatter(links, xd, core_d, one_d, two_d, three_d, sem_rs.at[0])
    rs_u = Scatter(links, xu, core_u, one_u, two_u, three_u, sem_rs.at[1])
    rs_0 = Scatter(links, x0, core_0, one_0, two_0, three_0, sem_rs.at[2])
    rs_1 = Scatter(links, x1, core_1, one_1, two_1, three_1, sem_rs.at[3])
    rs_2 = Scatter(links, x2, core_2, one_2, two_2, three_2, sem_rs.at[4])
    ag_d = Gather(links, df, sem_ag.at[0])
    ag_c = Gather(links, cf, sem_ag.at[1])
    sums = [AllSum(links, near.at[i], far.at[i], sem_ar.at[i]) for i in range(5)]

    first_row = (me["z"] * 32 + me["y"] * 8 + me["c"] * 4 + me["x"]) * ROWS
    splits = [split_ref[l : l + 1, :SPLITS] for l in range(LEVELS)]
    seed = [[seed_ref[l, j : j + 1, :] - first_row for j in range(2)] for l in range(LEVELS)]

    def place(sign):
        @pl.loop(0, tiles)
        def _(i):
            at = pl.ds(aligned(i * TILE, TILE), TILE)
            row = lax.broadcasted_iota(I32, (TILE, SPLITS), 0) + i * TILE
            for l in range(LEVELS):
                value = jnp.where(row == seed[l][0], 1.0, 0.0) + jnp.where(row == seed[l][1], sign, 0.0)
                oh[at, l * SPLITS : (l + 1) * SPLITS] = value.astype(BF)

    place(-1.0)

    @pl.loop(0, tiles)
    def _(i):
        fetch(i).wait()
        at = pl.ds(aligned(i * TILE, TILE), TILE)
        high, low = two(jnp.transpose(e_ref[at, :]))
        eth[:, at] = high
        etl[:, at] = low

    def as_they_lie(i, carry):
        at = pl.ds(aligned(i * TILE, TILE), TILE)
        rows = e_ref[at, :]
        high, low = two(rows)
        eh[at, :] = high
        el[at, :] = low
        squares = jnp.sum(rows * rows, axis=1, keepdims=True)
        sq[at, :] = squares
        return tuple(
            carry[l] + jnp.sum(oh[at, l * SPLITS : (l + 1) * SPLITS].astype(F32) * squares, axis=0, keepdims=True)
            for l in range(LEVELS)
        )

    def select_rows(dst, q):
        at = slice(256 * q, 256 * q + 256)
        dst[at, :] = dot(eth[at, :], oh[...]) + dot(etl[at, :], oh[...])

    select_rows(xd, 0)
    pl.semaphore_wait(barrier, len(peers))
    rs_d.start_core(0)
    select_rows(xd, 1)
    rs_d.start_core(1)
    select_rows(xd, 2)
    rs_d.start_core(2)
    rs_d.start_one(0)

    lines = [splits[0], splits[1], seed_ref[0, 0:1, :], seed_ref[0, 1:2, :], seed_ref[1, 0:1, :], seed_ref[1, 1:2, :]]
    lines = [line.astype(F32) for line in lines] + [jnp.zeros((TILE - 6, SPLITS), F32)]
    colt[...] = jnp.transpose(jnp.concatenate(lines, axis=0))
    memc[...] = jnp.transpose(
        jnp.concatenate([mem_ref[...].astype(F32), jnp.zeros((TILE - LEVELS, ROWS), F32)], axis=0)
    )
    col = [colt[:, k : k + 1] for k in range(6)]
    kid1 = splits[1]
    a1, s10, s11 = pick(kid1 >> 1, [col[0], col[2], col[3]])
    odd1 = (kid1 & 1) == 1
    seed1 = jnp.where(odd1, s11, s10) - first_row
    kid2 = splits[2]
    mid2, s20, s21 = pick(kid2 >> 1, [col[1], col[4], col[5]])
    odd2 = (kid2 & 1) == 1
    seed2 = jnp.where(odd2, s21, s20) - first_row
    a2, t20, t21 = pick(mid2 >> 1, [col[0], col[2], col[3]])
    odd20 = (mid2 & 1) == 1
    seed20 = jnp.where(odd20, t21, t20) - first_row
    rs_d.start_one(1)
    rs_d.start_one(2)
    norms = lax.fori_loop(0, tiles, as_they_lie, (jnp.zeros((1, SPLITS), F32),) * LEVELS)
    sums[0].start(list(norms))

    root_copy.wait()

    @pl.loop(0, KIDS // TILE)
    def _(i):
        at = pl.ds(aligned(i * TILE, TILE), TILE)
        rows = root_ref[at, :]
        high, low = two(rows)
        rh[at, :] = high
        rl[at, :] = low
        roott[:, at] = jnp.transpose(rows)

    place(1.0)
    sums[0].middle()
    rs_d.every(rs_d.start_two)
    select_rows(xu, 0)
    rs_d.every(rs_d.start_three)
    select_rows(xu, 1)
    own_d = []
    for q in range(PARTS):
        own_d.append(rs_d.finish(q))
        ag_d.start_two(q, own_d[q])
    own_d = jnp.concatenate(own_d, axis=0)
    select_rows(xu, 2)
    ag_d.start_one()
    norm = sums[0].finish()
    ag_d.start_core()
    for q in range(PARTS):
        rs_u.start_core(q)

    for q in range(PARTS):
        ag_d.wait(q)
        for i in range(2):
            at = slice(256 * q + 128 * i, 256 * q + 128 * (i + 1))
            high, low = two(df[at, :])
            dh[at, :] = high
            dl[at, :] = low

    def products(first):
        @pl.loop(first, first + 2)
        def _(i):
            at = pl.ds(aligned(i * 256, 256), 256)
            proj[at, :] = dot(eh[at, :], dh[...]) + dot(eh[at, :], dl[...]) + dot(el[at, :], dh[...])

    products(0)
    rs_u.every(rs_u.start_one)
    products(2)

    def root_products(levels, indices):
        cols = slice(levels[0] * SPLITS, (levels[-1] + 1) * SPLITS)

        def body(i, carry):
            at = pl.ds(aligned(i * TILE, TILE), TILE)
            value = dot(rh[at, :], dh[:, cols]) + dot(rh[at, :], dl[:, cols]) + dot(rl[at, :], dh[:, cols])
            row = lax.broadcasted_iota(I32, (TILE, SPLITS), 0) + i * TILE
            return tuple(
                carry[k] + jnp.sum(jnp.where(row == index, value[:, k * SPLITS : (k + 1) * SPLITS], 0.0), axis=0, keepdims=True)
                for k, index in enumerate(indices)
            )

        return lax.fori_loop(0, KIDS // TILE, body, (jnp.zeros((1, SPLITS), F32),) * len(levels))

    along0 = root_products([0], [splits[0]])[0]

    scale = 0.5 / float(WIDTH) ** 0.5

    def level(l, offset, chains):
        zero = jnp.zeros((1, SPLITS), F32)
        chains = [(cluster.astype(F32), odd, seed_row, ahead) for cluster, odd, seed_row, ahead in chains]
        own = splits[l].astype(F32)

        def body(i, carry):
            at = pl.ds(aligned(i * TILE, TILE), TILE)
            member = memc[at, l : l + 1]
            value = proj[at, l * SPLITS : (l + 1) * SPLITS] + offset
            gap = jnp.sum(jnp.where(member == own, value, 0.0), axis=1, keepdims=True)
            first = lax.logistic(gap * scale)
            second = 1.0 - first
            firsts[at, :] = first
            out = []
            row = lax.broadcasted_iota(I32, (TILE, SPLITS), 0) + i * TILE
            for cluster, odd, seed_row, ahead in chains:
                weight = jnp.where(member == cluster, jnp.where(odd, second, first), 0.0)
                both = weight + jnp.where(row == seed_row, 0.5, 0.0)
                out.append(jnp.sum(both * proj[at, ahead * SPLITS : (ahead + 1) * SPLITS], axis=0, keepdims=True))
                out.append(jnp.sum(weight, axis=0, keepdims=True))
            return tuple(a + b for a, b in zip(carry, out))

        return list(lax.fori_loop(0, tiles, body, (zero,) * (2 * len(chains))))

    def weigh(l):
        zero = jnp.zeros((1, SPLITS), F32)
        own = splits[l].astype(F32)

        def body(i, carry):
            at = pl.ds(aligned(i * TILE, TILE), TILE)
            hit = memc[at, l : l + 1] == own
            first = firsts[at, :]
            squares = sq[at, :]
            inside = jnp.sum(jnp.where(hit, 1.0, 0.0), axis=1, keepdims=True)
            cwbuf[at, l : l + 1] = first * inside
            out = []
            for j, part in enumerate((first, 1.0 - first)):
                weight = jnp.where(hit, part, 0.0)
                high, low = two(weight)
                w_hi[at, j * SPLITS : (j + 1) * SPLITS] = high
                w_lo[at, j * SPLITS : (j + 1) * SPLITS] = low
                out.append(jnp.sum(weight, axis=0, keepdims=True))
                out.append(jnp.sum(weight * squares, axis=0, keepdims=True))
            return tuple(a + b for a, b in zip(carry, out))

        return list(lax.fori_loop(0, tiles, body, (zero,) * 4))

    def add_up(dst, q, j):
        at, cols = slice(256 * q, 256 * q + 256), slice(SPLITS * j, SPLITS * j + SPLITS)
        high = w_hi[:, cols]
        dst[at, cols] = dot(eth[at, :], high) + dot(etl[at, :], high) + dot(eth[at, :], w_lo[:, cols])

    offset = -0.5 * along0 - 0.25 * norm[0:1, :]
    got0 = level(0, offset, [(a1, odd1, seed1, 1), (a2, odd20, seed20, 2)])
    sums[1].start(got0)
    tally0 = weigh(0)
    add_up(x0, 0, 0)
    sums[1].middle()
    along1, along2 = root_products([1, 2], [a1, a2])
    add_up(x0, 0, 1)
    rs_0.start_core(0)
    for q in (1, 2):
        for j in (0, 1):
            add_up(x0, q, j)
        rs_0.start_core(q)
    got0 = sums[1].finish()

    parent = (got0[0:1, :] + 0.5 * along1) / (got0[1:2, :] + 1.0)
    offset = -0.5 * parent - 0.25 * norm[1:2, :]
    got1 = level(1, offset, [(mid2, odd2, seed2, 2)])
    sums[2].start(got1 + tally0)
    tally1 = weigh(1)
    rs_u.every(rs_u.start_two)
    add_up(x1, 0, 0)
    sums[2].middle()
    add_up(x1, 0, 1)
    rs_1.start_core(0)
    add_up(x1, 1, 0)
    rs_0.every(rs_0.start_one)
    add_up(x1, 1, 1)
    rs_1.start_core(1)
    add_up(x1, 2, 0)
    add_up(x1, 2, 1)
    rs_1.start_core(2)
    got1 = sums[2].finish()

    rs_1.every(rs_1.start_one)
    older = (got0[2:3, :] + 0.5 * along2) / (got0[3:4, :] + 1.0)
    parent = (got1[0:1, :] + 0.5 * older) / (got1[1:2, :] + 1.0)
    offset = -0.5 * parent - 0.25 * norm[2:3, :]
    level(2, offset, [])
    tally2 = weigh(2)
    sums[3].start(tally1 + tally2)
    for q in range(PARTS):
        for j in (0, 1):
            add_up(x2, q, j)
        rs_2.start_core(q)
        if q:
            rs_2.start_one(q - 1)
    rs_2.start_one(2)
    sums[3].middle()
    rs_u.every(rs_u.start_three)
    rs_0.every(rs_0.start_two)
    rs_1.every(rs_1.start_two)
    cw_ref[...] = jnp.transpose(cwbuf[...])[0:LEVELS]
    own_u = rs_u.finish_all()
    rs_2.every(rs_2.start_two)
    rs_0.every(rs_0.start_three)
    rs_1.every(rs_1.start_three)

    def flat(kid):
        return (kid & 1) * SPLITS + (kid >> 1)

    def seeds_of(l, parent):
        up = own_u[:, l * SPLITS : (l + 1) * SPLITS]
        diff = own_d[:, l * SPLITS : (l + 1) * SPLITS]
        return 0.5 * jnp.concatenate([parent + 0.5 * (up + diff), parent + 0.5 * (up - diff)], axis=1)

    def parents(from_, kid):
        line = lax.broadcasted_iota(I32, (KIDS, SPLITS), 0)
        return jnp.dot(from_, jnp.where(line == kid, 1.0, 0.0).astype(F32), precision=HIGH, preferred_element_type=F32)

    def counts_of(got):
        return jnp.concatenate([got[0:1, :], got[2:3, :]], axis=1)

    def error_of(count, centre, mine):
        return 0.25 * jnp.sum(count * centre * centre - 2.0 * centre * mine, axis=0, keepdims=True)

    roots = jnp.concatenate([roott[pl.ds(aligned(own_row(links, q), 8), 8), :] for q in range(PARTS)], axis=0)
    got0 = got1[2:6, :]
    n0 = counts_of(got0)
    own_0 = rs_0.finish_all()
    c1 = (own_0 + seeds_of(0, parents(roots, splits[0]))) / (n0 + 1.0)
    err0 = error_of(n0, c1, own_0)
    got2 = sums[3].finish()
    got1, got2 = got2[0:4, :], got2[4:8, :]
    n1, n2 = counts_of(got1), counts_of(got2)
    rs_2.every(rs_2.start_three)
    own_1 = rs_1.finish_all()
    c2 = (own_1 + seeds_of(1, parents(c1, flat(kid1)))) / (n1 + 1.0)
    err1 = error_of(n1, c2, own_1)
    seeds2 = seeds_of(2, parents(c2, flat(kid2)))
    part, err2 = [], 0.0
    for q in range(PARTS):
        mine = rs_2.finish(q)
        centre = (mine + seeds2[8 * q : 8 * q + 8]) / (n2 + 1.0)
        ag_c.start_two(q, centre)
        err2 = err2 + error_of(n2, centre, mine)
    sums[4].start([e[:, j * SPLITS : (j + 1) * SPLITS] for e in (err0, err1, err2) for j in range(2)])
    ag_c.start_one()
    sums[4].middle()
    ag_c.start_core()

    copies = []

    def weave(q, half):
        w = 2 * q + half
        rows = cf[pl.ds(aligned(TILE * w, TILE), TILE), :]
        for j in range(2):
            woven[w, pl.ds(j, SPLITS, stride=2), :] = jnp.transpose(rows[:, j * SPLITS : (j + 1) * SPLITS])
        copy = pltpu.make_async_copy(
            woven.at[w], cent_hbm.at[:, pl.ds(aligned(w * TILE, TILE), TILE)], sem_out.at[len(copies)]
        )
        copy.start()
        copies.append(copy)

    c = me["c"]
    for q in range(PARTS):
        weave(q, c)
    total = sums[4].finish()
    lines = []
    for l, (got, n) in enumerate(((got0, n0), (got1, n1), (got2, n2))):
        energy = jnp.concatenate([got[1:2, :], got[3:4, :]], axis=1)
        error = jnp.concatenate([total[2 * l : 2 * l + 1, :], total[2 * l + 1 : 2 * l + 2, :]], axis=1)
        lines.append((energy + error) / ((n + 1.0) * WIDTH))
    lines.append(jnp.zeros((8 - LEVELS, KIDS), F32))
    line = lax.broadcasted_iota(I32, (KIDS, KIDS), 0)
    kid = lax.broadcasted_iota(I32, (KIDS, KIDS), 1)
    order = jnp.where(line == flat(kid), 1.0, 0.0).astype(F32)
    spread_ref[...] = jnp.dot(
        jnp.concatenate(lines, axis=0), order, precision=HIGH, preferred_element_type=F32
    )[0:LEVELS]
    for q in range(PARTS):
        ag_c.wait(q)
        weave(q, 1 - c)
    for copy in copies:
        copy.wait()
    links.drain()


def scratch_shapes():
    vm = pltpu.VMEM
    widths = (WIDTH, WIDTH, KIDS, KIDS, KIDS)
    shapes = [
        vm((ROWS, WIDTH), F32), vm((KIDS, WIDTH), F32),
        vm((ROWS, WIDTH), BF), vm((ROWS, WIDTH), BF), vm((WIDTH, ROWS), BF), vm((WIDTH, ROWS), BF),
        vm((KIDS, WIDTH), BF), vm((KIDS, WIDTH), BF), vm((WIDTH, KIDS), F32),
        vm((ROWS, WIDTH), BF), vm((ROWS, KIDS), BF),
        vm((WIDTH, WIDTH), BF), vm((WIDTH, WIDTH), BF), vm((ROWS, WIDTH), F32),
        vm((ROWS, 1), F32), vm((ROWS, TILE), F32), vm((SPLITS, TILE), F32), vm((ROWS, TILE), F32), vm((ROWS, 1), F32),
    ]
    shapes += [vm((WIDTH, n), F32) for n in widths]
    shapes += [vm((WIDTH, WIDTH), F32), vm((WIDTH, KIDS), F32)]
    shapes += [vm((PARTS, 128, n), F32) for n in widths]
    shapes += [vm((PARTS, 3, 32, n), F32) for n in widths]
    shapes += [vm((PARTS, 3, 8, n), F32) for n in widths]
    shapes += [vm((PARTS, 4, 8, n), F32) for n in widths]
    dma = pltpu.SemaphoreType.DMA
    shapes += [vm((5, 8, 8, SPLITS), F32), vm((5, 16, 8, SPLITS), F32)]
    shapes += [vm((WIDTH // TILE, KIDS, TILE), F32)]
    shapes += [dma((5, 2, PARTS, 10)), dma((2, 2, PARTS, 7)), dma((5, 2, 22)), dma((ROWS // TILE + 1,)), dma((6,))]
    return shapes


def hand_on_kernel(cent_ref, spread_ref, cw_ref, cent_out, spread_out, cw_out):
    cent_out[...] = cent_ref[...]

    @pl.when(pl.program_id(0) == 0)
    def _():
        spread_out[...] = spread_ref[...]
        cw_out[...] = cw_ref[...]


def hand_on(*results):
    steps = 2
    specs = [
        pl.BlockSpec((KIDS // steps, WIDTH), lambda i: (i, 0)),
        pl.BlockSpec((LEVELS, KIDS), lambda i: (0, 0)),
        pl.BlockSpec((LEVELS, ROWS), lambda i: (0, 0)),
    ]
    return pl.pallas_call(
        hand_on_kernel,
        grid=(steps,),
        out_shape=tuple(jax.ShapeDtypeStruct(r.shape, r.dtype) for r in results),
        in_specs=specs,
        out_specs=tuple(specs),
        compiler_params=pltpu.CompilerParams(vmem_limit_bytes=66_000_000),
    )(*results)


def on_device(embeddings, root_centroids, member_ids, split_order, seed_rows):
    vmem = pl.BlockSpec(memory_space=pltpu.VMEM)
    hbm = pl.BlockSpec(memory_space=pl.ANY)
    results = pl.pallas_call(
        kernel,
        out_shape=(
            jax.ShapeDtypeStruct((KIDS, WIDTH), F32),
            jax.ShapeDtypeStruct((LEVELS, KIDS), F32),
            jax.ShapeDtypeStruct((LEVELS, ROWS), F32),
        ),
        in_specs=[hbm, hbm, vmem, vmem, vmem],
        out_specs=(hbm, vmem, vmem),
        scratch_shapes=scratch_shapes(),
        compiler_params=pltpu.CompilerParams(
            collective_id=0, has_side_effects=True, vmem_limit_bytes=66_000_000
        ),
    )(embeddings, root_centroids, member_ids, split_order, seed_rows.transpose(0, 2, 1))
    return hand_on(*results)


def solution(mesh):
    split = Mesh(mesh.devices.reshape(4, 4, 2, 4), AXES)
    everywhere = ("z", "y", "c", "x")
    in_specs = (P(everywhere, None), P(), P(None, everywhere), P(), P())
    out_specs = (P(), P(), P(None, everywhere))
    return jax.shard_map(on_device, mesh=split, in_specs=in_specs, out_specs=out_specs, check_vma=False)
```
